32 devices in a mesh: clip: 8 (over z, x), seq: 4 (over y, core).
Axes of the slice: x: 2, y: 2, z: 4, core: 2. Of those that a mesh axis runs over, the one named last changes fastest.
Arguments:
- clip_tokens: bfloat16 [8, 4, 196, 1024], P('clip', 'seq'), may hold values from -6 to 6
- attn_gain: float32 [1024], replicated, may hold values from 0.5 to 1.5
- qkv_weight: bfloat16 [1024, 3072], replicated, may hold values from -0.1875 to 0.1875
- out_weight: bfloat16 [1024, 1024], replicated, may hold values from -0.1875 to 0.1875
- head_gain: float32 [1024], replicated, may hold values from 0.5 to 1.5
- gloss_weight: bfloat16 [1024, 1200], replicated, may hold values from -1.5 to 1.5
- gloss_targets: int32 [8, 2], P('clip'), may hold values from 1 to 1199
- target_lengths: int32 [8], P('clip'), may hold values from 1 to 2, as said below
Outputs:
- clip_loss: float32 [8], P('clip')
- grad_tokens: bfloat16 [8, 4, 196, 1024], P('clip', 'seq')
- grad_attn_gain: float32 [1024], P('seq')
- grad_qkv: float32 [1024, 3072], P('seq')
- grad_out: float32 [1024, 1024], P('seq')
- grad_head_gain: float32 [1024], P('seq')
- grad_gloss: float32 [1024, 1200], P('seq')
The draws below stay inside these ranges and needn't reach their ends.
Inputs may be any that keep to these rules, and one draw needn't show every extreme that they name: `target_lengths`: some clip has exactly 2 glosses, and some has half of 2, rounded up.
All inputs are finite; a program needn't handle non-finite values.
Results may differ from the reference program's by a relative error of at most 0.02.
Values may be sent and summed in bfloat16 or wider, within the bound.
A program may use at most 128 MiB of HBM per device.

```python
import jax
import jax.numpy as jnp
from jax import lax

D = 1024
H = 16
HD = 64
V = 1200
P_SIZE = 196
FRAMES = 4
CLIPS = 8
LMAX = 2


def draw_target_lengths(key, part):
    key_base, key_top = jax.random.split(key, 2)
    lowest = (LMAX + 1) // 2
    drawn = jax.random.randint(key_base, (CLIPS,), lowest, LMAX + 1, dtype=jnp.int32)
    top_at = jax.random.randint(key_top, (), 0, CLIPS, dtype=jnp.int32)
    drawn = drawn.at[top_at].set(LMAX)
    drawn = drawn.at[(top_at + 1) % CLIPS].set(lowest)
    return drawn


def place_ends(array, key, smallest, largest):
    shape = array.shape
    place = [jax.random.randint(jax.random.fold_in(key, axis), (), 0, shape[axis]) for axis in range(len(shape))]
    array = array.at[tuple(place)].set(smallest)
    longest = shape.index(max(shape))
    place[longest] = (place[longest] + 1) % shape[longest]
    return array.at[tuple(place)].set(largest)


def block_levels(key, dims, cuts, low, high):
    gain, own = 1.0, jax.random.fold_in(key, 6)
    for dim, shards_of in cuts:
        steps = jnp.exp(jax.random.uniform(jax.random.fold_in(own, dim), (shards_of,), jnp.float32, low / len(cuts), high / len(cuts)))
        gain = gain * jnp.repeat(steps, dims[dim] // shards_of).reshape([-1 if axis == dim else 1 for axis in range(len(dims))])
    return gain


def scatter_about(key, dims, scale, limit, shards=(), kind=jnp.bfloat16):
    level = block_levels(key, dims, shards, -0.22, 0.18) if shards else 1.0
    result = jax.random.normal(key, dims, jnp.float32) * scale * level
    return jnp.minimum(jnp.maximum(result, -limit), limit).astype(kind)


def setup_inputs(seed: int = 0) -> dict:
    splits = jax.random.split(jax.random.key(seed), 9)
    clip_tokens = scatter_about(splits[0], (CLIPS, FRAMES, P_SIZE, D), 1.0, 6.0, ((0, 8), (1, 4)))
    attn_gain = jnp.clip(1.0 + 0.1 * jax.random.normal(splits[1], (D,), jnp.float32), 0.5, 1.5)
    qkv_weight = scatter_about(splits[2], (D, 3 * D), D ** -0.5, 0.1875)
    out_weight = scatter_about(splits[3], (D, D), D ** -0.5, 0.1875)
    head_gain = jnp.clip(1.0 + 0.1 * jax.random.normal(splits[4], (D,), jnp.float32), 0.5, 1.5)
    gloss_weight = scatter_about(splits[5], (D, V), 0.094, 1.5)
    gloss_targets = place_ends(jax.random.randint(splits[6], (CLIPS, LMAX), 1, V), jax.random.fold_in(splits[6], 1), 1, V - 1).astype(jnp.int32)
    target_lengths = draw_target_lengths(jax.random.fold_in(splits[8], 71), 0)
    return {"clip_tokens": clip_tokens, "attn_gain": attn_gain, "qkv_weight": qkv_weight, "out_weight": out_weight, "head_gain": head_gain, "gloss_weight": gloss_weight, "gloss_targets": gloss_targets, "target_lengths": target_lengths}


epsilon = 1e-06
very_low = -10000.0

def layer_norm(inputs, gain_vec):
    centred = inputs - lax.optimization_barrier(jnp.mean(inputs, axis=-1, keepdims=True))
    inv_scale = lax.rsqrt(lax.optimization_barrier(jnp.mean(centred * centred, axis=-1, keepdims=True)) + epsilon)
    normed = centred * inv_scale
    return (normed * gain_vec, normed, inv_scale)

def norm_back(grad_out, normed, inv_scale, gain_vec):
    scaled = grad_out * gain_vec
    centred = scaled - lax.optimization_barrier(jnp.mean(scaled, axis=-1, keepdims=True))
    grad_in = inv_scale * (centred - normed * lax.optimization_barrier(jnp.mean(scaled * normed, axis=-1, keepdims=True)))
    return (grad_in, lax.optimization_barrier(jnp.sum(grad_out * normed, axis=0)))

def attend(head_parts):
    queries = head_parts[:, :, :, 0].astype(jnp.float32)
    key_rows = head_parts[:, :, :, 1].astype(jnp.float32)
    val_rows = head_parts[:, :, :, 2].astype(jnp.float32)
    scores = jnp.einsum('tnhe,snhe->nhts', queries, key_rows) * HD ** (-0.5)
    raised = jnp.exp(scores)
    attn_probs = raised / lax.optimization_barrier(jnp.sum(raised, axis=-1, keepdims=True))
    probs_low = attn_probs.astype(jnp.bfloat16)
    attended = jnp.einsum('nhts,snhe->tnhe', probs_low.astype(jnp.float32), val_rows)
    return (attended.astype(jnp.bfloat16), attn_probs)

def attend_back(head_parts, attn_probs, grad_att):
    queries = head_parts[:, :, :, 0].astype(jnp.float32)
    key_rows = head_parts[:, :, :, 1].astype(jnp.float32)
    val_rows = head_parts[:, :, :, 2].astype(jnp.float32)
    grad_wide = grad_att.astype(jnp.float32)
    probs_low = attn_probs.astype(jnp.bfloat16).astype(jnp.float32)
    grad_vals = jnp.einsum('nhts,tnhe->snhe', probs_low, grad_wide)
    grad_probs = jnp.einsum('tnhe,snhe->nhts', grad_wide, val_rows)
    grad_scores = attn_probs * (grad_probs - lax.optimization_barrier(jnp.sum(grad_probs * attn_probs, axis=-1, keepdims=True))) * HD ** (-0.5)
    scores_low = grad_scores.astype(jnp.bfloat16).astype(jnp.float32)
    grad_query = jnp.einsum('nhts,snhe->tnhe', scores_low, key_rows)
    grad_keys = jnp.einsum('nhts,tnhe->snhe', scores_low, queries)
    return jnp.stack([grad_query, grad_keys, grad_vals], axis=3).astype(jnp.bfloat16)

def ctc_loss(logits, labels, length):
    label_cap = labels.shape[0]
    log_probs = logits - jnp.log(lax.optimization_barrier(jnp.sum(jnp.exp(logits), axis=1, keepdims=True)))
    states = jnp.arange(2 * label_cap + 1, dtype=jnp.int32)
    label_slot = jnp.clip((states - 1) // 2, 0, label_cap - 1).astype(jnp.int32)
    extended = jnp.where(states % 2 == 1, jnp.take(labels, label_slot), 0).astype(jnp.int32)
    before = jnp.concatenate([jnp.full((2,), -1, jnp.int32), extended[:-2]])
    may_skip = (states % 2 == 1) & (extended != before)
    usable = states < 2 * length + 1
    emitted = jnp.take(log_probs, extended, axis=1)
    start_alpha = jnp.where((states < 2) & usable, emitted[0], very_low)

    def advance(alphas, emit_row):
        from_one = jnp.concatenate([jnp.full((1,), very_low, alphas.dtype), alphas[:-1]])
        from_two = jnp.concatenate([jnp.full((2,), very_low, alphas.dtype), alphas[:-2]])
        from_two = jnp.where(may_skip, from_two, very_low)
        updated = jnp.logaddexp(jnp.logaddexp(alphas, from_one), from_two) + emit_row
        return (jnp.where(usable, updated, very_low), None)
    alphas, trace_out = lax.scan(advance, start_alpha, emitted[1:])
    ending = jnp.logaddexp(jnp.take(alphas, 2 * length), jnp.take(alphas, 2 * length - 1))
    return -ending / length.astype(logits.dtype)

def clip_pass(tokens, labels, length, attn_gain, qkv_weight, out_weight, head_gain, gloss_weight):
    frame_count, patches, model_width = tokens.shape
    local_rows = tokens.reshape(frame_count * patches, model_width).astype(jnp.float32)
    normed_tok, plain_one, inv_one = layer_norm(local_rows, attn_gain)
    normed_low = normed_tok.astype(jnp.bfloat16)
    qkv_rows = jnp.dot(normed_low, qkv_weight, preferred_element_type=jnp.float32).astype(jnp.bfloat16)
    head_parts = qkv_rows.reshape(frame_count, patches, H, 3, HD)
    attended, attn_probs = attend(head_parts)
    att_rows = attended.reshape(frame_count * patches, model_width)
    mixed_rows = local_rows + jnp.dot(att_rows, out_weight, preferred_element_type=jnp.float32)
    pooled = lax.optimization_barrier(jnp.mean(mixed_rows.reshape(frame_count, patches, model_width), axis=1))
    frame_full, plain_two, inv_two = layer_norm(pooled, head_gain)
    frame_rows = frame_full.astype(jnp.bfloat16)
    logits = jnp.dot(frame_rows, gloss_weight, preferred_element_type=jnp.float32)

    def clip_objective(logit_rows):
        return ctc_loss(logit_rows, labels, length)
    clip_value, loss_back = jax.vjp(clip_objective, logits)
    grad_logits, = loss_back(jnp.ones_like(clip_value))
    grad_low = grad_logits.astype(jnp.bfloat16)
    grad_gloss = jnp.dot(frame_rows.T, grad_low, preferred_element_type=jnp.float32)
    grad_frame = jnp.dot(grad_low, gloss_weight.T, preferred_element_type=jnp.float32)
    grad_pooled, grad_head = norm_back(grad_frame, plain_two, inv_two, head_gain)
    grad_mixed = jnp.broadcast_to((grad_pooled / patches)[:, None, :], (frame_count, patches, model_width))
    grad_mixed = grad_mixed.reshape(frame_count * patches, model_width)
    mixed_low = grad_mixed.astype(jnp.bfloat16)
    grad_outw = jnp.dot(att_rows.T, mixed_low, preferred_element_type=jnp.float32)
    grad_att = jnp.dot(mixed_low, out_weight.T, preferred_element_type=jnp.float32).astype(jnp.bfloat16)
    grad_parts = attend_back(head_parts, attn_probs, grad_att.reshape(frame_count, patches, H, HD))
    grad_qkv_rows = grad_parts.reshape(frame_count * patches, 3 * model_width)
    grad_qkvw = jnp.dot(normed_low.T, grad_qkv_rows, preferred_element_type=jnp.float32)
    grad_normed = jnp.dot(grad_qkv_rows, qkv_weight.T, preferred_element_type=jnp.float32)
    grad_local, grad_attn = norm_back(grad_normed, plain_one, inv_one, attn_gain)
    grad_tokens = ((grad_local + grad_mixed) * patches).astype(jnp.bfloat16)
    grad_tokens = grad_tokens.reshape(frame_count, patches, model_width)
    return (clip_value, grad_tokens, (grad_attn, grad_qkvw, grad_outw, grad_head, grad_gloss))

def reference(clip_tokens, attn_gain, qkv_weight, out_weight, head_gain, gloss_weight, gloss_targets, target_lengths):
    model_width = clip_tokens.shape[3]
    starting = (jnp.zeros((model_width,), jnp.float32), jnp.zeros(qkv_weight.shape, jnp.float32), jnp.zeros(out_weight.shape, jnp.float32), jnp.zeros((model_width,), jnp.float32), jnp.zeros(gloss_weight.shape, jnp.float32))

    def one_clip(totals, inputs):
        tokens, labels, length = inputs
        clip_value, grad_tokens, grads = clip_pass(tokens, labels, length, attn_gain, qkv_weight, out_weight, head_gain, gloss_weight)
        return (jax.tree.map(jnp.add, totals, grads), (clip_value, grad_tokens))
    totals, outputs = lax.scan(one_clip, starting, (clip_tokens, gloss_targets, target_lengths))
    return (outputs[0], outputs[1], totals[0], totals[1], totals[2], totals[3], totals[4])
```

```python
import functools

import jax
import jax.numpy as jnp
from jax import lax
from jax.experimental import pallas as pl
from jax.experimental.pallas import tpu as pltpu
from jax.sharding import PartitionSpec as P

H = 16
HD = 64
SCALE = HD ** (-0.5)

epsilon = 1e-06
very_low = -10000.0
f32 = jnp.float32
bf16 = jnp.bfloat16


def up(value, step):
    return -(-value // step) * step


def dot(left, right, dims=((1,), (0,))):
    return lax.dot_general(left, right, (dims, ((), ())), preferred_element_type=f32)


def spread(head_lanes, width, first, frame):
    row = lax.broadcasted_iota(jnp.int32, (head_lanes, width), 0)
    col = lax.broadcasted_iota(jnp.int32, (head_lanes, width), 1) + first
    return jnp.where(row == frame * H + lax.shift_right_logical(col, 6), 1.0, 0.0).astype(bf16)


def by_head(rows, head_lanes):
    count, width = rows.shape
    row = lax.broadcasted_iota(jnp.int32, (H, width), 0)
    col = lax.broadcasted_iota(jnp.int32, (H, width), 1)
    own = row == lax.shift_right_logical(col, 6)
    parts = [
        jnp.where(own, jnp.broadcast_to(rows[t : t + 1], (H, width)), 0.0) for t in range(count)
    ]
    if head_lanes > count * H:
        parts.append(jnp.zeros((head_lanes - count * H, width), f32))
    return jnp.concatenate(parts, axis=0)


def low_lanes(rows):
    return lax.broadcasted_iota(jnp.int32, (rows, 128), 1) < HD


def forward_kernel(x_ref, gain_ref, w_ref, q_ref, k_ref, v_ref, p_ref, low_ref, norm_ref, inv_ref, sum_ref):
    frames, here, width = x_ref.shape
    rows = frames * here
    head_lanes = p_ref.shape[1]
    x = x_ref[...].reshape(rows, width).astype(f32)
    centred = x - jnp.mean(x, axis=1, keepdims=True)
    inv = lax.rsqrt(jnp.mean(centred * centred, axis=1, keepdims=True) + epsilon)
    normed = centred * inv
    norm_ref[...] = normed
    inv_ref[...] = jnp.broadcast_to(inv, (rows, 128))
    low_ref[...] = (normed * gain_ref[...]).astype(bf16)
    low = low_lanes(rows)
    for pair in range(H // 2):
        y = dot(low_ref[...], w_ref[:, pair * 384 : (pair + 1) * 384])
        a, b, c = y[:, :128], y[:, 128:256], y[:, 256:]
        at = slice(pair * 128, (pair + 1) * 128)
        q_ref[:, at] = jnp.where(low, a, b).astype(bf16)
        k_ref[:, at] = pltpu.roll(jnp.where(low, c, a), HD, 1).astype(bf16)
        v_ref[:, at] = jnp.where(low, b, c).astype(bf16)
    keys = k_ref[...].astype(f32).reshape(frames, here, width)
    scores = jnp.zeros((rows, head_lanes), f32)
    for t in range(frames):
        q_t = q_ref[t * here : (t + 1) * here, :].astype(f32)
        prod = (keys * q_t[None]).reshape(rows, width).astype(bf16)
        scores += dot(prod, spread(head_lanes, width, 0, t), ((1,), (1,)))
    raised = jnp.exp(scores * SCALE).reshape(frames, here, head_lanes)
    probs = raised / jnp.sum(raised, axis=0, keepdims=True)
    probs = probs.reshape(rows, head_lanes)
    p_ref[...] = probs
    mixed = dot(probs.astype(bf16), v_ref[...], ((0,), (0,)))
    row = lax.broadcasted_iota(jnp.int32, (H, width), 0)
    col = lax.broadcasted_iota(jnp.int32, (H, width), 1)
    own = row == lax.shift_right_logical(col, 6)
    sum_ref[...] = jnp.zeros_like(sum_ref)
    for t in range(frames):
        sum_ref[0, t : t + 1, :] = jnp.sum(x[t * here : (t + 1) * here], axis=0, keepdims=True)
        sum_ref[1, t : t + 1, :] = jnp.sum(
            jnp.where(own, mixed[t * H : (t + 1) * H], 0.0), axis=0, keepdims=True
        )


def add_log(left, right):
    top = jnp.maximum(left, right)
    return top + jnp.log(1.0 + jnp.exp(-jnp.abs(left - right)))


def middle_kernel(
    patches, frames, labels_ref, length_ref, sums_ref, wo_ref, gain_ref, wg_ref,
    loss_ref, frame_ref, gl_ref, head_ref, mix_ref, low_ref, ga_ref, att_ref,
):
    total = jnp.sum(sums_ref[...], axis=0)
    sum_tok, sum_att = total[0], total[1]
    att_ref[...] = sum_att
    hi = sum_att.astype(bf16)
    lo = (sum_att - hi.astype(f32)).astype(bf16)
    pooled = (sum_tok + dot(hi, wo_ref[...]) + dot(lo, wo_ref[...])) * (1.0 / patches)
    centred = pooled - jnp.mean(pooled, axis=1, keepdims=True)
    inv = lax.rsqrt(jnp.mean(centred * centred, axis=1, keepdims=True) + epsilon)
    plain = centred * inv
    frame = (plain * gain_ref[...]).astype(bf16)
    frame_ref[...] = frame
    logits = dot(frame, wg_ref[...])
    padded, vocab = logits.shape
    raised = jnp.exp(logits)
    denom = jnp.sum(raised, axis=1, keepdims=True)
    soft = raised / denom
    logs = logits - jnp.log(denom)
    cap = labels_ref.shape[1]
    length = length_ref[0]
    lane = lax.broadcasted_iota(jnp.int32, (1, 128), 1)
    gloss = lax.broadcasted_iota(jnp.int32, (padded, vocab), 1)

    def pick(label):
        return jnp.sum(jnp.where(gloss == label, logs, 0.0), axis=1, keepdims=True)

    wide = lax.broadcasted_iota(jnp.int32, (padded, 128), 1)
    emitted = jnp.where((wide & 1) == 0, pick(0), 0.0)
    skip = lane < 0
    for i in range(cap):
        label = labels_ref[0, i]
        emitted = jnp.where(wide == 2 * i + 1, pick(label), emitted)
        before = labels_ref[0, i - 1] if i else -1
        skip = skip | ((lane == 2 * i + 1) & (label != before))
    usable = lane < 2 * length + 1
    start = (lane < 2) & usable
    alphas = jnp.where(start, emitted[0:1], very_low)
    kept = []
    for t in range(1, frames):
        one = jnp.where(lane < 1, very_low, pltpu.roll(alphas, 1, 1))
        two = jnp.where(skip, pltpu.roll(alphas, 2, 1), very_low)
        outer = add_log(add_log(alphas, one), two)
        kept.append((jnp.exp(alphas - outer), jnp.exp(one - outer), jnp.exp(two - outer)))
        alphas = jnp.where(usable, outer + emitted[t : t + 1], very_low)
    last = jnp.sum(jnp.where(lane == 2 * length, alphas, 0.0), axis=1, keepdims=True)
    prior = jnp.sum(jnp.where(lane == 2 * length - 1, alphas, 0.0), axis=1, keepdims=True)
    ending = add_log(last, prior)
    share = 1.0 / length.astype(f32)
    loss_ref[...] = jnp.broadcast_to(-ending * share, (8, 128))
    grad = jnp.where(
        (lane == 2 * length) | (lane == 2 * length - 1), -share * jnp.exp(alphas - ending), 0.0
    )
    row = lax.broadcasted_iota(jnp.int32, (padded, 128), 0)
    emit_grad = jnp.zeros((padded, 128), f32)
    for t in range(frames - 1, 0, -1):
        grad = jnp.where(usable, grad, 0.0)
        emit_grad = jnp.where(row == t, grad, emit_grad)
        w_own, w_one, w_two = kept[t - 1]
        from_one = jnp.where(lane < 1, 0.0, grad * w_one)
        from_two = jnp.where(skip, grad * w_two, 0.0)
        from_two = jnp.where(lane < 2, 0.0, from_two)
        grad = grad * w_own + pltpu.roll(from_one, 127, 1) + pltpu.roll(from_two, 126, 1)
    emit_grad = jnp.where(row == 0, jnp.where(start, grad, 0.0), emit_grad)
    blank = jnp.sum(jnp.where((wide & 1) == 0, emit_grad, 0.0), axis=1, keepdims=True)
    d_logs = jnp.where(gloss == 0, blank, 0.0)
    for i in range(cap):
        part = jnp.sum(jnp.where(wide == 2 * i + 1, emit_grad, 0.0), axis=1, keepdims=True)
        d_logs = d_logs + jnp.where(gloss == labels_ref[0, i], part, 0.0)
    d_logits = d_logs - soft * jnp.sum(emit_grad, axis=1, keepdims=True)
    gl = d_logits.astype(bf16)
    gl_ref[...] = gl
    grad_frame = dot(gl, wg_ref[...], ((1,), (1,)))
    head_ref[...] = jnp.broadcast_to(jnp.sum(grad_frame * plain, axis=0, keepdims=True), head_ref.shape)
    scaled = grad_frame * gain_ref[...]
    grad_pooled = inv * (
        scaled
        - jnp.mean(scaled, axis=1, keepdims=True)
        - plain * jnp.mean(scaled * plain, axis=1, keepdims=True)
    )
    grad_mixed = grad_pooled * (1.0 / patches)
    mix_ref[...] = grad_mixed
    mixed_low = grad_mixed.astype(bf16)
    low_ref[...] = mixed_low
    ga_ref[...] = dot(mixed_low, wo_ref[...], ((1,), (1,))).astype(bf16)


def backward_kernel(
    patches, frames, here, q_ref, k_ref, v_ref, p_ref, low_ref, norm_ref, inv_ref, ga_ref, mix_ref,
    gain_ref, w_ref, gt_ref, dw_ref, cols_ref, qk_ref,
):
    rows, width = q_ref.shape
    head_lanes = p_ref.shape[1]
    ga = by_head(ga_ref[...].astype(f32)[:frames], head_lanes).astype(bf16)
    probs = p_ref[...]
    probs_low = probs.astype(bf16)
    grad_probs = dot(v_ref[...], ga, ((1,), (1,)))
    inner = jnp.sum((grad_probs * probs).reshape(frames, here, head_lanes), axis=0, keepdims=True)
    grad_scores = probs.reshape(frames, here, head_lanes) * (
        grad_probs.reshape(frames, here, head_lanes) - inner
    )
    scores_low = (grad_scores.reshape(rows, head_lanes) * SCALE).astype(bf16)
    low = low_lanes(rows)
    for pair in range(H // 2):
        at = slice(pair * 128, (pair + 1) * 128)
        keys = k_ref[:, at].astype(f32).reshape(frames, here, 128)
        grad_keys = jnp.zeros((frames, here, 128), f32)
        queries = []
        for t in range(frames):
            wide = dot(scores_low, spread(head_lanes, 128, pair * 128, t)).reshape(frames, here, 128)
            queries.append(jnp.sum(wide * keys, axis=0))
            q_t = q_ref[t * here : (t + 1) * here, at].astype(f32)
            grad_keys += wide * q_t[None]
        gq = jnp.concatenate(queries, axis=0)
        gk = pltpu.roll(grad_keys.reshape(rows, 128), HD, 1)
        gv = dot(probs_low, ga[:, at])
        qk_ref[:, pair * 256 : pair * 256 + 128] = gq.astype(bf16)
        qk_ref[:, pair * 256 + 128 : pair * 256 + 256] = gk.astype(bf16)
        a = jnp.where(low, gq, gk).astype(bf16)
        b = jnp.where(low, gv, gq).astype(bf16)
        c = jnp.where(low, gk, gv).astype(bf16)
        part = dot(
            jnp.concatenate([a, b, c], axis=1), w_ref[:, pair * 384 : (pair + 1) * 384], ((1,), (1,))
        )
        if pair == 0:
            grad_normed = part
        else:
            grad_normed += part
    tokens_low = low_ref[...]
    chunk = 512
    for start in range(0, 2 * width, chunk):
        dw_ref[:, start : start + chunk] = dot(
            tokens_low, qk_ref[:, start : start + chunk], ((0,), (0,))
        ).astype(bf16)
    cols_ref[:, :head_lanes] = dot(tokens_low, probs_low, ((0,), (0,))).astype(bf16)
    normed = norm_ref[...]
    gain_part = (grad_normed * normed).astype(bf16)
    cols_ref[:, head_lanes:] = dot(gain_part, jnp.ones((rows, 128), bf16), ((0,), (0,))).astype(bf16)
    scaled = grad_normed * gain_ref[...]
    back = inv_ref[:, :1] * (
        scaled
        - jnp.mean(scaled, axis=1, keepdims=True)
        - normed * jnp.mean(scaled * normed, axis=1, keepdims=True)
    )
    for t in range(frames):
        gt_ref[t] = ((back[t * here : (t + 1) * here] + mix_ref[t : t + 1, :]) * patches).astype(bf16)


def final_kernel(
    frames, qk_ref, cols_ref, att_ref, mix_ref, frame_ref, gl_ref, ga_ref, head_ref,
    qkv_out, out_out, gloss_out, head_out, gain_out,
):
    clips, block, lanes = cols_ref.shape
    head_lanes = lanes - 128
    out_out[...] = dot(att_ref[...], mix_ref[...], ((0,), (0,)))
    gloss_out[...] = dot(frame_ref[...], gl_ref[...], ((0,), (0,)))
    head_out[...] = jnp.sum(head_ref[...].astype(f32), axis=0, keepdims=True)
    gain_out[...] = jnp.sum(cols_ref[:, :, head_lanes:].astype(f32), axis=0)
    values = None
    for c in range(clips):
        ga = by_head(ga_ref[c].astype(f32)[:frames], head_lanes).astype(bf16)
        part = dot(cols_ref[c, :, :head_lanes], ga)
        values = part if values is None else values + part
    low = low_lanes(block)
    for pair in range(H // 2):
        q = qk_ref[:, pair * 256 : pair * 256 + 128].astype(f32)
        k = qk_ref[:, pair * 256 + 128 : pair * 256 + 256].astype(f32)
        v = values[:, pair * 128 : (pair + 1) * 128]
        qkv_out[:, pair * 384 : pair * 384 + 128] = jnp.where(low, q, k)
        qkv_out[:, pair * 384 + 128 : pair * 384 + 256] = jnp.where(low, v, q)
        qkv_out[:, pair * 384 + 256 : pair * 384 + 384] = jnp.where(low, k, v)


def params():
    return pltpu.CompilerParams(vmem_limit_bytes=56 << 20)


def shape(dims, kind):
    return jax.ShapeDtypeStruct(dims, kind)


VM = pl.BlockSpec(memory_space=pltpu.VMEM)
SM = pl.BlockSpec(memory_space=pltpu.SMEM)


def per_device(
    clip_tokens, attn_gain, qkv_weight, out_weight, head_gain, gloss_weight, gloss_targets, target_lengths
):
    seq_count = lax.axis_size("seq")
    clips = lax.axis_size("clip")
    me = lax.axis_index("seq")
    local, patches, width = clip_tokens.shape[1:]
    vocab = gloss_weight.shape[1]
    frames = local * seq_count
    here = up(-(-patches // seq_count), 16)
    rows = frames * here
    head_lanes = up(frames * H, 128)
    padded = up(frames, 8)
    block = width // seq_count
    gain_row = attn_gain.reshape(1, width)

    own = jnp.pad(clip_tokens[0], ((0, 0), (0, here * seq_count - patches), (0, 0)))
    x = lax.all_to_all(own, "seq", split_axis=1, concat_axis=0, tiled=True)
    q, k, v, probs, low, normed, inv, sums = pl.pallas_call(
        forward_kernel,
        out_shape=(
            shape((rows, width), bf16),
            shape((rows, width), bf16),
            shape((rows, width), bf16),
            shape((rows, head_lanes), f32),
            shape((rows, width), bf16),
            shape((rows, width), f32),
            shape((rows, 128), f32),
            shape((2, padded, width), f32),
        ),
        in_specs=[VM] * 3,
        out_specs=(VM,) * 8,
        compiler_params=params(),
        name="forward",
    )(x, gain_row, qkv_weight)
    all_sums = lax.all_gather(sums, "seq", axis=0)
    loss, frame_rows, gl, head_part, grad_mixed, mixed_low, ga, sum_att = pl.pallas_call(
        functools.partial(middle_kernel, patches, frames),
        out_shape=(
            shape((8, 128), f32),
            shape((padded, width), bf16),
            shape((padded, vocab), bf16),
            shape((8, width), f32),
            shape((padded, width), f32),
            shape((padded, width), bf16),
            shape((padded, width), bf16),
            shape((padded, width), f32),
        ),
        in_specs=[SM, SM] + [VM] * 4,
        out_specs=(VM,) * 8,
        compiler_params=params(),
        name="middle",
    )(gloss_targets, target_lengths, all_sums, out_weight, head_gain.reshape(1, width), gloss_weight)

    def cut(array):
        return lax.dynamic_slice_in_dim(array, me * block, block, 1)

    head8 = jnp.concatenate([head_part[:1], jnp.zeros((padded - 1, width), f32)], axis=0)
    packed = jnp.concatenate(
        [mixed_low, ga, gl, cut(frame_rows), cut(sum_att).astype(bf16), cut(head8).astype(bf16)], axis=1
    )
    gathered = lax.all_gather(packed, "clip", axis=0)
    gt, dw, cols = pl.pallas_call(
        functools.partial(backward_kernel, patches, frames, here),
        out_shape=(
            shape((frames, here, width), bf16),
            shape((width, 2 * width), bf16),
            shape((width, head_lanes + 128), bf16),
        ),
        in_specs=[VM] * 11,
        out_specs=(VM,) * 3,
        scratch_shapes=[pltpu.VMEM((rows, 2 * width), bf16)],
        compiler_params=params(),
        name="backward",
    )(q, k, v, probs, low, normed, inv, ga, grad_mixed, gain_row, qkv_weight)
    dw_own = lax.psum_scatter(dw, "seq", scatter_dimension=0, tiled=True)
    cols_own = lax.psum_scatter(cols, "seq", scatter_dimension=0, tiled=True)
    dw_sum = lax.psum(dw_own, "clip")
    cols_all = lax.all_gather(cols_own, "clip", axis=0)
    back = lax.all_to_all(gt, "seq", split_axis=0, concat_axis=1, tiled=True)
    grad_tokens = back[None, :, :patches]

    def part(start, size):
        return gathered[:, :, start : start + size]

    flat = clips * padded
    at = 2 * width + vocab
    qkv_share, out_share, gloss_share, head_share, gain_share = pl.pallas_call(
        functools.partial(final_kernel, frames),
        out_shape=(
            shape((block, 3 * width), f32),
            shape((block, width), f32),
            shape((block, vocab), f32),
            shape((1, block), f32),
            shape((block, 128), f32),
        ),
        in_specs=[VM] * 8,
        out_specs=(VM,) * 5,
        compiler_params=params(),
        name="final",
    )(
        dw_sum,
        cols_all,
        part(at + block, block).reshape(flat, block),
        part(0, width).reshape(flat, width),
        part(at, block).reshape(flat, block),
        part(2 * width, vocab).reshape(flat, vocab),
        part(width, width),
        part(at + 2 * block, block).reshape(flat, block),
    )
    return (
        loss[0, :1],
        grad_tokens,
        gain_share[:, 0],
        qkv_share,
        out_share,
        head_share[0],
        gloss_share,
    )


def solution(mesh):
    in_specs = (P("clip", "seq", None, None), P(), P(), P(), P(), P(), P("clip", None), P("clip"))
    out_specs = (
        P("clip"),
        P("clip", "seq", None, None),
        P("seq"),
        P("seq", None),
        P("seq", None),
        P("seq"),
        P("seq", None),
    )
    return jax.shard_map(
        per_device, mesh=mesh, in_specs=in_specs, out_specs=out_specs, check_vma=False
    )
```

```python
import functools

import jax
import jax.numpy as jnp
from jax import lax
from jax.experimental import pallas as pl
from jax.experimental.pallas import tpu as pltpu
from jax.sharding import PartitionSpec as P

H = 16
HD = 64
SCALE = HD ** (-0.5)

epsilon = 1e-06
very_low = -10000.0
f32 = jnp.float32
bf16 = jnp.bfloat16


def up(value, step):
    return -(-value // step) * step


def dot(left, right, dims=((1,), (0,))):
    return lax.dot_general(left, right, (dims, ((), ())), preferred_element_type=f32)


def spread(head_lanes, width, first, frame):
    row = lax.broadcasted_iota(jnp.int32, (head_lanes, width), 0)
    col = lax.broadcasted_iota(jnp.int32, (head_lanes, width), 1) + first
    return jnp.where(row == frame * H + lax.shift_right_logical(col, 6), 1.0, 0.0).astype(bf16)


def by_head(rows, head_lanes):
    count, width = rows.shape
    row = lax.broadcasted_iota(jnp.int32, (H, width), 0)
    col = lax.broadcasted_iota(jnp.int32, (H, width), 1)
    own = row == lax.shift_right_logical(col, 6)
    parts = [
        jnp.where(own, jnp.broadcast_to(rows[t : t + 1], (H, width)), 0.0) for t in range(count)
    ]
    if head_lanes > count * H:
        parts.append(jnp.zeros((head_lanes - count * H, width), f32))
    return jnp.concatenate(parts, axis=0)


def low_lanes(rows):
    return lax.broadcasted_iota(jnp.int32, (rows, 128), 1) < HD


def forward_kernel(x_ref, gain_ref, w_ref, q_ref, k_ref, v_ref, p_ref, low_ref, norm_ref, inv_ref, sum_ref):
    frames, here, width = x_ref.shape
    rows = frames * here
    head_lanes = p_ref.shape[1]
    x = x_ref[...].reshape(rows, width).astype(f32)
    centred = x - jnp.mean(x, axis=1, keepdims=True)
    inv = lax.rsqrt(jnp.mean(centred * centred, axis=1, keepdims=True) + epsilon)
    normed = centred * inv
    norm_ref[...] = normed
    inv_ref[...] = jnp.broadcast_to(inv, (rows, 128))
    low_ref[...] = (normed * gain_ref[...]).astype(bf16)
    low = low_lanes(rows)
    for pair in range(H // 2):
        y = dot(low_ref[...], w_ref[:, pair * 384 : (pair + 1) * 384])
        a, b, c = y[:, :128], y[:, 128:256], y[:, 256:]
        at = slice(pair * 128, (pair + 1) * 128)
        q_ref[:, at] = jnp.where(low, a, b).astype(bf16)
        k_ref[:, at] = pltpu.roll(jnp.where(low, c, a), HD, 1).astype(bf16)
        v_ref[:, at] = jnp.where(low, b, c).astype(bf16)
    keys = k_ref[...].astype(f32).reshape(frames, here, width)
    scores = jnp.zeros((rows, head_lanes), f32)
    for t in range(frames):
        q_t = q_ref[t * here : (t + 1) * here, :].astype(f32)
        prod = (keys * q_t[None]).reshape(rows, width).astype(bf16)
        scores += dot(prod, spread(head_lanes, width, 0, t), ((1,), (1,)))
    raised = jnp.exp(scores * SCALE).reshape(frames, here, head_lanes)
    probs = raised / jnp.sum(raised, axis=0, keepdims=True)
    probs = probs.reshape(rows, head_lanes)
    p_ref[...] = probs
    mixed = dot(probs.astype(bf16), v_ref[...], ((0,), (0,)))
    row = lax.broadcasted_iota(jnp.int32, (H, width), 0)
    col = lax.broadcasted_iota(jnp.int32, (H, width), 1)
    own = row == lax.shift_right_logical(col, 6)
    sum_ref[...] = jnp.zeros_like(sum_ref)
    for t in range(frames):
        sum_ref[0, t : t + 1, :] = jnp.sum(x[t * here : (t + 1) * here], axis=0, keepdims=True)
        sum_ref[1, t : t + 1, :] = jnp.sum(
            jnp.where(own, mixed[t * H : (t + 1) * H], 0.0), axis=0, keepdims=True
        )


def add_log(left, right):
    top = jnp.maximum(left, right)
    return top + jnp.log(1.0 + jnp.exp(-jnp.abs(left - right)))


def middle_kernel(
    patches, frames, labels_ref, length_ref, sums_ref, wo_ref, gain_ref, wg_ref,
    loss_ref, frame_ref, gl_ref, head_ref, mix_ref, low_ref, ga_ref, att_ref,
):
    total = jnp.sum(sums_ref[...], axis=0)
    sum_tok, sum_att = total[0], total[1]
    att_ref[...] = sum_att
    hi = sum_att.astype(bf16)
    lo = (sum_att - hi.astype(f32)).astype(bf16)
    pooled = (sum_tok + dot(hi, wo_ref[...]) + dot(lo, wo_ref[...])) * (1.0 / patches)
    centred = pooled - jnp.mean(pooled, axis=1, keepdims=True)
    inv = lax.rsqrt(jnp.mean(centred * centred, axis=1, keepdims=True) + epsilon)
    plain = centred * inv
    frame = (plain * gain_ref[...]).astype(bf16)
    frame_ref[...] = frame
    logits = dot(frame, wg_ref[...])
    padded, vocab = logits.shape
    raised = jnp.exp(logits)
    denom = jnp.sum(raised, axis=1, keepdims=True)
    soft = raised / denom
    logs = logits - jnp.log(denom)
    cap = labels_ref.shape[1]
    length = length_ref[0]
    lane = lax.broadcasted_iota(jnp.int32, (1, 128), 1)
    gloss = lax.broadcasted_iota(jnp.int32, (padded, vocab), 1)

    def pick(label):
        return jnp.sum(jnp.where(gloss == label, logs, 0.0), axis=1, keepdims=True)

    wide = lax.broadcasted_iota(jnp.int32, (padded, 128), 1)
    emitted = jnp.where((wide & 1) == 0, pick(0), 0.0)
    skip = lane < 0
    for i in range(cap):
        label = labels_ref[0, i]
        emitted = jnp.where(wide == 2 * i + 1, pick(label), emitted)
        before = labels_ref[0, i - 1] if i else -1
        skip = skip | ((lane == 2 * i + 1) & (label != before))
    usable = lane < 2 * length + 1
    start = (lane < 2) & usable
    alphas = jnp.where(start, emitted[0:1], very_low)
    kept = []
    for t in range(1, frames):
        one = jnp.where(lane < 1, very_low, pltpu.roll(alphas, 1, 1))
        two = jnp.where(skip, pltpu.roll(alphas, 2, 1), very_low)
        outer = add_log(add_log(alphas, one), two)
        kept.append((jnp.exp(alphas - outer), jnp.exp(one - outer), jnp.exp(two - outer)))
        alphas = jnp.where(usable, outer + emitted[t : t + 1], very_low)
    last = jnp.sum(jnp.where(lane == 2 * length, alphas, 0.0), axis=1, keepdims=True)
    prior = jnp.sum(jnp.where(lane == 2 * length - 1, alphas, 0.0), axis=1, keepdims=True)
    ending = add_log(last, prior)
    share = 1.0 / length.astype(f32)
    loss_ref[...] = jnp.broadcast_to(-ending * share, (8, 128))
    grad = jnp.where(
        (lane == 2 * length) | (lane == 2 * length - 1), -share * jnp.exp(alphas - ending), 0.0
    )
    row = lax.broadcasted_iota(jnp.int32, (padded, 128), 0)
    emit_grad = jnp.zeros((padded, 128), f32)
    for t in range(frames - 1, 0, -1):
        grad = jnp.where(usable, grad, 0.0)
        emit_grad = jnp.where(row == t, grad, emit_grad)
        w_own, w_one, w_two = kept[t - 1]
        from_one = jnp.where(lane < 1, 0.0, grad * w_one)
        from_two = jnp.where(skip, grad * w_two, 0.0)
        from_two = jnp.where(lane < 2, 0.0, from_two)
        grad = grad * w_own + pltpu.roll(from_one, 127, 1) + pltpu.roll(from_two, 126, 1)
    emit_grad = jnp.where(row == 0, jnp.where(start, grad, 0.0), emit_grad)
    blank = jnp.sum(jnp.where((wide & 1) == 0, emit_grad, 0.0), axis=1, keepdims=True)
    d_logs = jnp.where(gloss == 0, blank, 0.0)
    for i in range(cap):
        part = jnp.sum(jnp.where(wide == 2 * i + 1, emit_grad, 0.0), axis=1, keepdims=True)
        d_logs = d_logs + jnp.where(gloss == labels_ref[0, i], part, 0.0)
    d_logits = d_logs - soft * jnp.sum(emit_grad, axis=1, keepdims=True)
    gl = d_logits.astype(bf16)
    gl_ref[...] = gl
    grad_frame = dot(gl, wg_ref[...], ((1,), (1,)))
    head_ref[...] = jnp.broadcast_to(jnp.sum(grad_frame * plain, axis=0, keepdims=True), head_ref.shape)
    scaled = grad_frame * gain_ref[...]
    grad_pooled = inv * (
        scaled
        - jnp.mean(scaled, axis=1, keepdims=True)
        - plain * jnp.mean(scaled * plain, axis=1, keepdims=True)
    )
    grad_mixed = grad_pooled * (1.0 / patches)
    mix_ref[...] = grad_mixed
    mixed_low = grad_mixed.astype(bf16)
    low_ref[...] = mixed_low
    ga_ref[...] = dot(mixed_low, wo_ref[...], ((1,), (1,))).astype(bf16)


def backward_kernel(
    patches, frames, here, q_ref, k_ref, v_ref, p_ref, low_ref, norm_ref, inv_ref, ga_ref, mix_ref,
    gain_ref, w_ref, gt_ref, dw_ref, cols_ref, qk_ref,
):
    rows, width = q_ref.shape
    head_lanes = p_ref.shape[1]
    ga = by_head(ga_ref[...].astype(f32)[:frames], head_lanes).astype(bf16)
    probs = p_ref[...]
    probs_low = probs.astype(bf16)
    grad_probs = dot(v_ref[...], ga, ((1,), (1,)))
    inner = jnp.sum((grad_probs * probs).reshape(frames, here, head_lanes), axis=0, keepdims=True)
    grad_scores = probs.reshape(frames, here, head_lanes) * (
        grad_probs.reshape(frames, here, head_lanes) - inner
    )
    scores_low = (grad_scores.reshape(rows, head_lanes) * SCALE).astype(bf16)
    low = low_lanes(rows)
    for pair in range(H // 2):
        at = slice(pair * 128, (pair + 1) * 128)
        keys = k_ref[:, at].astype(f32).reshape(frames, here, 128)
        grad_keys = jnp.zeros((frames, here, 128), f32)
        queries = []
        for t in range(frames):
            wide = dot(scores_low, spread(head_lanes, 128, pair * 128, t)).reshape(frames, here, 128)
            queries.append(jnp.sum(wide * keys, axis=0))
            q_t = q_ref[t * here : (t + 1) * here, at].astype(f32)
            grad_keys += wide * q_t[None]
        gq = jnp.concatenate(queries, axis=0)
        gk = pltpu.roll(grad_keys.reshape(rows, 128), HD, 1)
        gv = dot(probs_low, ga[:, at])
        qk_ref[:, pair * 256 : pair * 256 + 128] = gq.astype(bf16)
        qk_ref[:, pair * 256 + 128 : pair * 256 + 256] = gk.astype(bf16)
        a = jnp.where(low, gq, gk).astype(bf16)
        b = jnp.where(low, gv, gq).astype(bf16)
        c = jnp.where(low, gk, gv).astype(bf16)
        part = dot(
            jnp.concatenate([a, b, c], axis=1), w_ref[:, pair * 384 : (pair + 1) * 384], ((1,), (1,))
        )
        if pair == 0:
            grad_normed = part
        else:
            grad_normed += part
    tokens_low = low_ref[...]
    chunk = 512
    for start in range(0, 2 * width, chunk):
        dw_ref[:, start : start + chunk] = dot(
            tokens_low, qk_ref[:, start : start + chunk], ((0,), (0,))
        ).astype(bf16)
    coefs = dot(tokens_low, probs_low, ((0,), (0,)))
    normed = norm_ref[...]
    gain_part = (grad_normed * normed).astype(bf16)
    gain_cols = dot(gain_part, jnp.ones((rows, 128), bf16), ((0,), (0,)))
    if frames * H < head_lanes:
        lane = lax.broadcasted_iota(jnp.int32, (width, 128), 1)
        tail = head_lanes - 128
        if tail:
            cols_ref[:, :tail] = coefs[:, :tail].astype(bf16)
        cols_ref[:, tail:] = jnp.where(lane < frames * H - tail, coefs[:, tail:], gain_cols).astype(bf16)
    else:
        cols_ref[:, :head_lanes] = coefs.astype(bf16)
        cols_ref[:, head_lanes:] = gain_cols.astype(bf16)
    scaled = grad_normed * gain_ref[...]
    back = inv_ref[:, :1] * (
        scaled
        - jnp.mean(scaled, axis=1, keepdims=True)
        - normed * jnp.mean(scaled * normed, axis=1, keepdims=True)
    )
    for t in range(frames):
        gt_ref[t] = ((back[t * here : (t + 1) * here] + mix_ref[t : t + 1, :]) * patches).astype(bf16)


def final_kernel(
    frames, qk_ref, cols_ref, att_ref, mix_ref, frame_ref, gl_ref, ga_ref, head_ref,
    qkv_out, out_out, gloss_out, head_out, gain_out,
):
    clips, block, lanes = cols_ref.shape
    head_lanes = up(frames * H, 128)
    out_out[...] = dot(att_ref[...], mix_ref[...], ((0,), (0,)))
    gloss_out[...] = dot(frame_ref[...], gl_ref[...], ((0,), (0,)))
    head_out[...] = jnp.sum(head_ref[...].astype(f32), axis=0, keepdims=True)
    gain_out[...] = jnp.sum(cols_ref[:, :, lanes - 128 :].astype(f32), axis=0)
    values = None
    for c in range(clips):
        ga = by_head(ga_ref[c].astype(f32)[:frames], head_lanes).astype(bf16)
        part = dot(cols_ref[c, :, :head_lanes], ga)
        values = part if values is None else values + part
    low = low_lanes(block)
    for pair in range(H // 2):
        q = qk_ref[:, pair * 256 : pair * 256 + 128].astype(f32)
        k = qk_ref[:, pair * 256 + 128 : pair * 256 + 256].astype(f32)
        v = values[:, pair * 128 : (pair + 1) * 128]
        qkv_out[:, pair * 384 : pair * 384 + 128] = jnp.where(low, q, k)
        qkv_out[:, pair * 384 + 128 : pair * 384 + 256] = jnp.where(low, v, q)
        qkv_out[:, pair * 384 + 256 : pair * 384 + 384] = jnp.where(low, k, v)


def exchange_scratch(seq_count, clips, block, width, lanes, chunk_count):
    pairs, half = seq_count // 2, clips // 2
    wide = 2 * width + lanes
    piece = 2 * width // clips
    sems = pltpu.SemaphoreType.DMA
    return [
        pltpu.VMEM((pairs, block, wide), bf16),
        pltpu.VMEM((pairs, block, wide), bf16),
        pltpu.VMEM((pairs - 1, block, wide), bf16),
        pltpu.VMEM((block, wide), bf16),
        pltpu.VMEM((block, width), bf16),
        pltpu.VMEM((block, width), bf16),
        pltpu.VMEM((half - 1, block, piece), bf16),
        sems((2, seq_count - 1)),
        sems((2, half)),
        sems((2, chunk_count, 2 * pairs)),
        sems((2, chunk_count, pairs - 1)),
        sems((2, chunk_count)),
        sems((2, chunk_count, half - 1)),
        sems((2, chunk_count, half - 1)),
        sems((2, chunk_count, half - 1)),
        sems((2, chunk_count, 2)),
    ]


def exchange_kernel(
    chunk_count, dw_ref, cols_ref, rows_ref, gt_ref, sum_ref, all_cols_ref, all_rows_ref, back_ref,
    core_in, core_sum, pair_in, seq_sum, x_in, x_sum, z_in,
    token_sem, row_sem, core_sem, pair_sem, x_sem, z_sem, zq_sem, zc_sem, xg_sem,
):
    seq_count, local = back_ref.shape[:2]
    half = all_cols_ref.shape[1]
    pairs = seq_count // 2
    block, full = sum_ref.shape
    width = full // 2
    piece = width // half
    size = block // chunk_count
    me = lax.axis_index("seq")
    clip = lax.axis_index("clip")
    core, hi = lax.rem(me, 2), me // 2
    x, z = lax.rem(clip, 2), clip // 2

    def at(clip_id, seq_id):
        return (clip_id, seq_id)

    sibling = at(clip, hi * 2 + (1 - core))
    x_peer = at(z * 2 + (1 - x), me)

    def z_peer(step):
        return at(lax.rem(z + step, half) * 2 + x, me)

    barrier = pltpu.get_barrier_semaphore()
    peers = [at(clip, lax.rem(me + step, seq_count)) for step in range(1, seq_count)]
    peers += [x_peer] + [z_peer(step) for step in range(1, half)]
    for peer in peers:
        pl.semaphore_signal(barrier, inc=1, device_id=peer, device_id_type=pl.DeviceIdType.MESH)
    pl.semaphore_wait(barrier, len(peers))

    started = []

    def send(src, dst, sems, index, peer):
        copy = pltpu.make_async_remote_copy(
            src_ref=src,
            dst_ref=dst,
            send_sem=sems.at[(0,) + index],
            recv_sem=sems.at[(1,) + index],
            device_id=peer,
            device_id_type=pl.DeviceIdType.MESH,
        )
        copy.start()
        started.append(copy)
        return copy

    waits = {}

    def rows(c):
        return pl.ds(c * size, size)

    def block_rows(index, c):
        return pl.ds(pl.multiple_of(index * block + c * size, 16), size)

    def half_cols(index):
        return pl.ds(pl.multiple_of(index * width, 128), width)

    def first(c):
        waits[1, c] = []
        for p in range(pairs):
            src = block_rows(p * 2 + (1 - core), c)
            waits[1, c] += [
                send(dw_ref.at[src], core_in.at[p, rows(c), pl.ds(0, full)], core_sem, (c, 2 * p), sibling),
                send(
                    cols_ref.at[src],
                    core_in.at[p, rows(c), pl.ds(full, cols_ref.shape[1])],
                    core_sem,
                    (c, 2 * p + 1),
                    sibling,
                ),
            ]

    def second(c):
        for copy in waits[1, c]:
            copy.wait_recv()
        for p in range(pairs):
            own = block_rows(p * 2 + core, c)
            core_sum[p, rows(c), :full] = dw_ref[own, :] + core_in[p, rows(c), :full]
            core_sum[p, rows(c), full:] = cols_ref[own, :] + core_in[p, rows(c), full:]
        waits[2, c] = [
            send(
                core_sum.at[lax.rem(hi + step, pairs), rows(c)],
                pair_in.at[step - 1, rows(c)],
                pair_sem,
                (c, step - 1),
                at(clip, lax.rem(hi + step, pairs) * 2 + core),
            )
            for step in range(1, pairs)
        ]

    def third(c):
        for copy in waits[2, c]:
            copy.wait_recv()
        total = core_sum[hi, rows(c)].astype(f32)
        for step in range(pairs - 1):
            total += pair_in[step, rows(c)].astype(f32)
        total = total.astype(bf16)
        seq_sum[rows(c)] = total
        all_cols_ref[x, z, rows(c)] = total[:, full:]
        waits[3, c] = [
            send(seq_sum.at[rows(c), half_cols(1 - x)], x_in.at[rows(c)], x_sem, (c,), x_peer)
        ]
        waits[5, c] = [
            send(
                all_cols_ref.at[x, z, rows(c)],
                all_cols_ref.at[x, z, rows(c)],
                zc_sem,
                (c, step - 1),
                z_peer(step),
            )
            for step in range(1, half)
        ]

    def fourth(c):
        for copy in waits[3, c]:
            copy.wait_recv()
        x_sum[rows(c)] = seq_sum[rows(c), half_cols(x)] + x_in[rows(c)]
        waits[4, c] = [
            send(
                x_sum.at[rows(c), pl.ds(pl.multiple_of(lax.rem(z + step, half) * piece, 128), piece)],
                z_in.at[step - 1, rows(c)],
                z_sem,
                (c, step - 1),
                z_peer(step),
            )
            for step in range(1, half)
        ]

    def fifth(c):
        for copy in waits[4, c]:
            copy.wait_recv()
        total = x_sum[rows(c), pl.ds(pl.multiple_of(z * piece, 128), piece)].astype(f32)
        for step in range(half - 1):
            total += z_in[step, rows(c)].astype(f32)
        own = pl.ds(pl.multiple_of(x * width + z * piece, 128), piece)
        sum_ref[rows(c), own] = total.astype(bf16)
        waits[5, c] += [
            send(
                sum_ref.at[rows(c), own], sum_ref.at[rows(c), own], zq_sem, (c, step - 1), z_peer(step)
            )
            for step in range(1, half)
        ]

    def sixth(c):
        for copy in waits[5, c]:
            copy.wait_recv()
        mine = (rows(c), half_cols(x))
        waits[6, c] = [
            send(sum_ref.at[mine], sum_ref.at[mine], xg_sem, (c, 0), x_peer),
            send(
                all_cols_ref.at[x, :, rows(c)], all_cols_ref.at[x, :, rows(c)], xg_sem, (c, 1), x_peer
            ),
        ]

    def seventh(c):
        for copy in waits[6, c]:
            copy.wait_recv()

    stages = [first, second, third, fourth, fifth, sixth, seventh]
    for c in range(chunk_count):
        first(c)
    all_rows_ref[x, z] = rows_ref[...]
    row_waits = [
        send(rows_ref, all_rows_ref.at[x, z], row_sem, (step - 1,), z_peer(step))
        for step in range(1, half)
    ]
    token_waits = []
    for step in range(1, seq_count):
        to = lax.rem(me + step, seq_count)
        token_waits.append(
            send(gt_ref.at[pl.ds(to * local, local)], back_ref.at[me], token_sem, (step - 1,), at(clip, to))
        )
    back_ref[me] = gt_ref[pl.ds(me * local, local)]
    for wave in range(1, chunk_count + len(stages) - 1):
        for c in range(chunk_count):
            if 1 <= wave - c < len(stages):
                stages[wave - c](c)
        if wave == 2:
            for copy in row_waits:
                copy.wait_recv()
            row_waits = [send(all_rows_ref.at[x], all_rows_ref.at[x], row_sem, (half - 1,), x_peer)]
    for copy in row_waits + token_waits:
        copy.wait_recv()
    for copy in started:
        copy.wait_send()


def params():
    return pltpu.CompilerParams(vmem_limit_bytes=56 << 20)


def shape(dims, kind):
    return jax.ShapeDtypeStruct(dims, kind)


VM = pl.BlockSpec(memory_space=pltpu.VMEM)
SM = pl.BlockSpec(memory_space=pltpu.SMEM)


def per_device(
    clip_tokens, attn_gain, qkv_weight, out_weight, head_gain, gloss_weight, gloss_targets, target_lengths
):
    seq_count = lax.axis_size("seq")
    clips = lax.axis_size("clip")
    me = lax.axis_index("seq")
    local, patches, width = clip_tokens.shape[1:]
    vocab = gloss_weight.shape[1]
    frames = local * seq_count
    here = up(-(-patches // seq_count), 16)
    rows = frames * here
    head_lanes = up(frames * H, 128)
    lanes = up(frames * H + 1, 128)
    padded = up(frames, 8)
    block = width // seq_count
    gain_row = attn_gain.reshape(1, width)

    own = jnp.pad(clip_tokens[0], ((0, 0), (0, here * seq_count - patches), (0, 0)))
    x = lax.all_to_all(own, "seq", split_axis=1, concat_axis=0, tiled=True)
    q, k, v, probs, low, normed, inv, sums = pl.pallas_call(
        forward_kernel,
        out_shape=(
            shape((rows, width), bf16),
            shape((rows, width), bf16),
            shape((rows, width), bf16),
            shape((rows, head_lanes), f32),
            shape((rows, width), bf16),
            shape((rows, width), f32),
            shape((rows, 128), f32),
            shape((2, padded, width), f32),
        ),
        in_specs=[VM] * 3,
        out_specs=(VM,) * 8,
        compiler_params=params(),
        name="forward",
    )(x, gain_row, qkv_weight)
    all_sums = lax.all_gather(sums, "seq", axis=0)
    loss, frame_rows, gl, head_part, grad_mixed, mixed_low, ga, sum_att = pl.pallas_call(
        functools.partial(middle_kernel, patches, frames),
        out_shape=(
            shape((8, 128), f32),
            shape((padded, width), bf16),
            shape((padded, vocab), bf16),
            shape((8, width), f32),
            shape((padded, width), f32),
            shape((padded, width), bf16),
            shape((padded, width), bf16),
            shape((padded, width), f32),
        ),
        in_specs=[SM, SM] + [VM] * 4,
        out_specs=(VM,) * 8,
        compiler_params=params(),
        name="middle",
    )(gloss_targets, target_lengths, all_sums, out_weight, head_gain.reshape(1, width), gloss_weight)

    def cut(array):
        return lax.dynamic_slice_in_dim(array, me * block, block, 1)

    head8 = jnp.concatenate([head_part[:1], jnp.zeros((padded - 1, width), f32)], axis=0)
    packed = jnp.concatenate(
        [mixed_low, ga, gl, cut(frame_rows), cut(sum_att).astype(bf16), cut(head8).astype(bf16)], axis=1
    )
    gt, dw, cols = pl.pallas_call(
        functools.partial(backward_kernel, patches, frames, here),
        out_shape=(
            shape((frames, here, width), bf16),
            shape((width, 2 * width), bf16),
            shape((width, lanes), bf16),
        ),
        in_specs=[VM] * 11,
        out_specs=(VM,) * 3,
        scratch_shapes=[pltpu.VMEM((rows, 2 * width), bf16)],
        compiler_params=params(),
        name="backward",
    )(q, k, v, probs, low, normed, inv, ga, grad_mixed, gain_row, qkv_weight)
    half = clips // 2
    chunk_count = 4
    dw_sum, cols_all, gathered, back = pl.pallas_call(
        functools.partial(exchange_kernel, chunk_count),
        out_shape=(
            shape((block, 2 * width), bf16),
            shape((2, half, block, lanes), bf16),
            shape((2, half) + packed.shape, bf16),
            shape((seq_count, local, here, width), bf16),
        ),
        in_specs=[VM] * 4,
        out_specs=(VM,) * 4,
        scratch_shapes=exchange_scratch(seq_count, clips, block, width, lanes, chunk_count),
        compiler_params=pltpu.CompilerParams(
            vmem_limit_bytes=56 << 20, collective_id=0, has_side_effects=True
        ),
        name="exchange",
    )(dw, cols, packed, gt)
    cols_all = cols_all.reshape(clips, block, lanes)
    gathered = gathered.reshape((clips,) + packed.shape)
    back = back.transpose(1, 0, 2, 3).reshape(local, seq_count * here, width)
    grad_tokens = back[None, :, :patches]

    def part(start, size):
        return gathered[:, :, start : start + size]

    flat = clips * padded
    at = 2 * width + vocab
    qkv_share, out_share, gloss_share, head_share, gain_share = pl.pallas_call(
        functools.partial(final_kernel, frames),
        out_shape=(
            shape((block, 3 * width), f32),
            shape((block, width), f32),
            shape((block, vocab), f32),
            shape((1, block), f32),
            shape((block, 128), f32),
        ),
        in_specs=[VM] * 8,
        out_specs=(VM,) * 5,
        compiler_params=params(),
        name="final",
    )(
        dw_sum,
        cols_all,
        part(at + block, block).reshape(flat, block),
        part(0, width).reshape(flat, width),
        part(at, block).reshape(flat, block),
        part(2 * width, vocab).reshape(flat, vocab),
        part(width, width),
        part(at + 2 * block, block).reshape(flat, block),
    )
    return (
        loss[0, :1],
        grad_tokens,
        gain_share[:, 127],
        qkv_share,
        out_share,
        head_share[0],
        gloss_share,
    )


def solution(mesh):
    in_specs = (P("clip", "seq", None, None), P(), P(), P(), P(), P(), P("clip", None), P("clip"))
    out_specs = (
        P("clip"),
        P("clip", "seq", None, None),
        P("seq"),
        P("seq", None),
        P("seq", None),
        P("seq"),
        P("seq", None),
    )
    return jax.shard_map(
        per_device, mesh=mesh, in_specs=in_specs, out_specs=out_specs, check_vma=False
    )
```

```python
import functools

import jax
import jax.numpy as jnp
from jax import lax
from jax.experimental import pallas as pl
from jax.experimental.pallas import tpu as pltpu
from jax.sharding import PartitionSpec as P

H = 16
HD = 64
SCALE = HD ** (-0.5)

epsilon = 1e-06
very_low = -10000.0
f32 = jnp.float32
bf16 = jnp.bfloat16


def up(value, step):
    return -(-value // step) * step


def dot(left, right, dims=((1,), (0,))):
    return lax.dot_general(left, right, (dims, ((), ())), preferred_element_type=f32)


def spread(head_lanes, width, first, frame):
    row = lax.broadcasted_iota(jnp.int32, (head_lanes, width), 0)
    col = lax.broadcasted_iota(jnp.int32, (head_lanes, width), 1) + first
    return jnp.where(row == frame * H + lax.shift_right_logical(col, 6), 1.0, 0.0).astype(bf16)


def by_head(rows, head_lanes):
    count, width = rows.shape
    row = lax.broadcasted_iota(jnp.int32, (H, width), 0)
    col = lax.broadcasted_iota(jnp.int32, (H, width), 1)
    own = row == lax.shift_right_logical(col, 6)
    parts = [
        jnp.where(own, jnp.broadcast_to(rows[t : t + 1], (H, width)), 0.0) for t in range(count)
    ]
    if head_lanes > count * H:
        parts.append(jnp.zeros((head_lanes - count * H, width), f32))
    return jnp.concatenate(parts, axis=0)


def low_lanes(rows):
    return lax.broadcasted_iota(jnp.int32, (rows, 128), 1) < HD


def forward_kernel(
    own_ref, gain_ref, w_hbm, q_ref, k_ref, v_ref, p_ref, low_ref, norm_ref, inv_ref, all_sums_ref,
    x_ref, w_ref, w_sem, token_sem, sums_sem,
):
    frames, here, width = x_ref.shape
    local = own_ref.shape[0]
    seq_count = frames // local
    me = lax.axis_index("seq")
    clip = lax.axis_index("clip")
    w_copy = pltpu.make_async_copy(w_hbm, w_ref, w_sem)
    w_copy.start()
    barrier = pltpu.get_barrier_semaphore()
    for step in range(1, seq_count):
        pl.semaphore_signal(
            barrier,
            inc=1,
            device_id=(clip, lax.rem(me + step, seq_count)),
            device_id_type=pl.DeviceIdType.MESH,
        )
    pl.semaphore_wait(barrier, seq_count - 1)

    def send(src, dst, sems, step):
        copy = pltpu.make_async_remote_copy(
            src_ref=src,
            dst_ref=dst,
            send_sem=sems.at[0, step - 1],
            recv_sem=sems.at[1, step - 1],
            device_id=(clip, lax.rem(me + step, seq_count)),
            device_id_type=pl.DeviceIdType.MESH,
        )
        copy.start()
        return copy

    def patch_rows(device):
        return pl.ds(pl.multiple_of(device * here, 16), here)

    mine = pl.ds(me * local, local)
    tokens = [
        send(own_ref.at[:, patch_rows(lax.rem(me + step, seq_count))], x_ref.at[mine], token_sem, step)
        for step in range(1, seq_count)
    ]
    x_ref[mine] = own_ref[:, patch_rows(me)]
    for copy in tokens:
        copy.wait_recv()
    rows = frames * here
    head_lanes = p_ref.shape[1]
    x = x_ref[...].reshape(rows, width).astype(f32)
    centred = x - jnp.mean(x, axis=1, keepdims=True)
    inv = lax.rsqrt(jnp.mean(centred * centred, axis=1, keepdims=True) + epsilon)
    normed = centred * inv
    norm_ref[...] = normed
    inv_ref[...] = jnp.broadcast_to(inv, (rows, 128))
    low_ref[...] = (normed * gain_ref[...]).astype(bf16)
    low = low_lanes(rows)
    w_copy.wait()
    for pair in range(H // 2):
        y = dot(low_ref[...], w_ref[:, pair * 384 : (pair + 1) * 384])
        a, b, c = y[:, :128], y[:, 128:256], y[:, 256:]
        at = slice(pair * 128, (pair + 1) * 128)
        q_ref[:, at] = jnp.where(low, a, b).astype(bf16)
        k_ref[:, at] = pltpu.roll(jnp.where(low, c, a), HD, 1).astype(bf16)
        v_ref[:, at] = jnp.where(low, b, c).astype(bf16)
    keys = k_ref[...].astype(f32).reshape(frames, here, width)
    scores = jnp.zeros((rows, head_lanes), f32)
    for t in range(frames):
        q_t = q_ref[t * here : (t + 1) * here, :].astype(f32)
        prod = (keys * q_t[None]).reshape(rows, width).astype(bf16)
        scores += dot(prod, spread(head_lanes, width, 0, t), ((1,), (1,)))
    raised = jnp.exp(scores * SCALE).reshape(frames, here, head_lanes)
    probs = raised / jnp.sum(raised, axis=0, keepdims=True)
    probs = probs.reshape(rows, head_lanes)
    p_ref[...] = probs
    mixed = dot(probs.astype(bf16), v_ref[...], ((0,), (0,)))
    row = lax.broadcasted_iota(jnp.int32, (H, width), 0)
    col = lax.broadcasted_iota(jnp.int32, (H, width), 1)
    own = row == lax.shift_right_logical(col, 6)
    padded = all_sums_ref.shape[2]
    blank = [jnp.zeros((padded - frames, width), f32)] if padded > frames else []
    tok = [jnp.sum(x[t * here : (t + 1) * here], axis=0, keepdims=True) for t in range(frames)]
    att = [
        jnp.sum(jnp.where(own, mixed[t * H : (t + 1) * H], 0.0), axis=0, keepdims=True)
        for t in range(frames)
    ]
    all_sums_ref[me, 0] = jnp.concatenate(tok + blank, axis=0)
    all_sums_ref[me, 1] = jnp.concatenate(att + blank, axis=0)
    sums = [send(all_sums_ref.at[me], all_sums_ref.at[me], sums_sem, step) for step in range(1, seq_count)]
    for copy in sums:
        copy.wait_recv()
    for copy in tokens + sums:
        copy.wait_send()


def add_log(left, right):
    top = jnp.maximum(left, right)
    return top + jnp.log(1.0 + jnp.exp(-jnp.abs(left - right)))


def middle_kernel(
    patches, frames, labels_ref, length_ref, sums_ref, wo_ref, gain_ref, wg_ref,
    loss_ref, frame_ref, gl_ref, head_ref, mix_ref, low_ref, ga_ref, att_ref,
):
    total = jnp.sum(sums_ref[...], axis=0)
    sum_tok, sum_att = total[0], total[1]
    att_ref[...] = sum_att
    hi = sum_att.astype(bf16)
    lo = (sum_att - hi.astype(f32)).astype(bf16)
    pooled = (sum_tok + dot(hi, wo_ref[...]) + dot(lo, wo_ref[...])) * (1.0 / patches)
    centred = pooled - jnp.mean(pooled, axis=1, keepdims=True)
    inv = lax.rsqrt(jnp.mean(centred * centred, axis=1, keepdims=True) + epsilon)
    plain = centred * inv
    frame = (plain * gain_ref[...]).astype(bf16)
    frame_ref[...] = frame
    logits = dot(frame, wg_ref[...])
    padded, vocab = logits.shape
    raised = jnp.exp(logits)
    denom = jnp.sum(raised, axis=1, keepdims=True)
    soft = raised / denom
    logs = logits - jnp.log(denom)
    cap = labels_ref.shape[1]
    length = length_ref[0]
    lane = lax.broadcasted_iota(jnp.int32, (1, 128), 1)
    gloss = lax.broadcasted_iota(jnp.int32, (padded, vocab), 1)

    def pick(label):
        return jnp.sum(jnp.where(gloss == label, logs, 0.0), axis=1, keepdims=True)

    wide = lax.broadcasted_iota(jnp.int32, (padded, 128), 1)
    emitted = jnp.where((wide & 1) == 0, pick(0), 0.0)
    skip = lane < 0
    for i in range(cap):
        label = labels_ref[0, i]
        emitted = jnp.where(wide == 2 * i + 1, pick(label), emitted)
        before = labels_ref[0, i - 1] if i else -1
        skip = skip | ((lane == 2 * i + 1) & (label != before))
    usable = lane < 2 * length + 1
    start = (lane < 2) & usable
    alphas = jnp.where(start, emitted[0:1], very_low)
    kept = []
    for t in range(1, frames):
        one = jnp.where(lane < 1, very_low, pltpu.roll(alphas, 1, 1))
        two = jnp.where(skip, pltpu.roll(alphas, 2, 1), very_low)
        outer = add_log(add_log(alphas, one), two)
        kept.append((jnp.exp(alphas - outer), jnp.exp(one - outer), jnp.exp(two - outer)))
        alphas = jnp.where(usable, outer + emitted[t : t + 1], very_low)
    last = jnp.sum(jnp.where(lane == 2 * length, alphas, 0.0), axis=1, keepdims=True)
    prior = jnp.sum(jnp.where(lane == 2 * length - 1, alphas, 0.0), axis=1, keepdims=True)
    ending = add_log(last, prior)
    share = 1.0 / length.astype(f32)
    loss_ref[...] = jnp.broadcast_to(-ending * share, (8, 128))
    grad = jnp.where(
        (lane == 2 * length) | (lane == 2 * length - 1), -share * jnp.exp(alphas - ending), 0.0
    )
    row = lax.broadcasted_iota(jnp.int32, (padded, 128), 0)
    emit_grad = jnp.zeros((padded, 128), f32)
    for t in range(frames - 1, 0, -1):
        grad = jnp.where(usable, grad, 0.0)
        emit_grad = jnp.where(row == t, grad, emit_grad)
        w_own, w_one, w_two = kept[t - 1]
        from_one = jnp.where(lane < 1, 0.0, grad * w_one)
        from_two = jnp.where(skip, grad * w_two, 0.0)
        from_two = jnp.where(lane < 2, 0.0, from_two)
        grad = grad * w_own + pltpu.roll(from_one, 127, 1) + pltpu.roll(from_two, 126, 1)
    emit_grad = jnp.where(row == 0, jnp.where(start, grad, 0.0), emit_grad)
    blank = jnp.sum(jnp.where((wide & 1) == 0, emit_grad, 0.0), axis=1, keepdims=True)
    d_logs = jnp.where(gloss == 0, blank, 0.0)
    for i in range(cap):
        part = jnp.sum(jnp.where(wide == 2 * i + 1, emit_grad, 0.0), axis=1, keepdims=True)
        d_logs = d_logs + jnp.where(gloss == labels_ref[0, i], part, 0.0)
    d_logits = d_logs - soft * jnp.sum(emit_grad, axis=1, keepdims=True)
    gl = d_logits.astype(bf16)
    gl_ref[...] = gl
    grad_frame = dot(gl, wg_ref[...], ((1,), (1,)))
    head_ref[...] = jnp.broadcast_to(jnp.sum(grad_frame * plain, axis=0, keepdims=True), head_ref.shape)
    scaled = grad_frame * gain_ref[...]
    grad_pooled = inv * (
        scaled
        - jnp.mean(scaled, axis=1, keepdims=True)
        - plain * jnp.mean(scaled * plain, axis=1, keepdims=True)
    )
    grad_mixed = grad_pooled * (1.0 / patches)
    mix_ref[...] = grad_mixed
    mixed_low = grad_mixed.astype(bf16)
    low_ref[...] = mixed_low
    ga_ref[...] = dot(mixed_low, wo_ref[...], ((1,), (1,))).astype(bf16)


def backward_kernel(
    patches, frames, here, q_ref, k_ref, v_ref, p_ref, low_ref, norm_ref, inv_ref, ga_ref, mix_ref,
    gain_ref, w_ref, gt_ref, dw_ref, cols_ref, qk_ref,
):
    rows, width = q_ref.shape
    head_lanes = p_ref.shape[1]
    ga = by_head(ga_ref[...].astype(f32)[:frames], head_lanes).astype(bf16)
    probs = p_ref[...]
    probs_low = probs.astype(bf16)
    grad_probs = dot(v_ref[...], ga, ((1,), (1,)))
    inner = jnp.sum((grad_probs * probs).reshape(frames, here, head_lanes), axis=0, keepdims=True)
    grad_scores = probs.reshape(frames, here, head_lanes) * (
        grad_probs.reshape(frames, here, head_lanes) - inner
    )
    scores_low = (grad_scores.reshape(rows, head_lanes) * SCALE).astype(bf16)
    low = low_lanes(rows)
    for pair in range(H // 2):
        at = slice(pair * 128, (pair + 1) * 128)
        keys = k_ref[:, at].astype(f32).reshape(frames, here, 128)
        grad_keys = jnp.zeros((frames, here, 128), f32)
        queries = []
        for t in range(frames):
            wide = dot(scores_low, spread(head_lanes, 128, pair * 128, t)).reshape(frames, here, 128)
            queries.append(jnp.sum(wide * keys, axis=0))
            q_t = q_ref[t * here : (t + 1) * here, at].astype(f32)
            grad_keys += wide * q_t[None]
        gq = jnp.concatenate(queries, axis=0)
        gk = pltpu.roll(grad_keys.reshape(rows, 128), HD, 1)
        gv = dot(probs_low, ga[:, at])
        qk_ref[:, pair * 256 : pair * 256 + 128] = gq.astype(bf16)
        qk_ref[:, pair * 256 + 128 : pair * 256 + 256] = gk.astype(bf16)
        a = jnp.where(low, gq, gk).astype(bf16)
        b = jnp.where(low, gv, gq).astype(bf16)
        c = jnp.where(low, gk, gv).astype(bf16)
        part = dot(
            jnp.concatenate([a, b, c], axis=1), w_ref[:, pair * 384 : (pair + 1) * 384], ((1,), (1,))
        )
        if pair == 0:
            grad_normed = part
        else:
            grad_normed += part
    tokens_low = low_ref[...]
    chunk = 512
    for start in range(0, 2 * width, chunk):
        dw_ref[:, start : start + chunk] = dot(
            tokens_low, qk_ref[:, start : start + chunk], ((0,), (0,))
        ).astype(bf16)
    coefs = dot(tokens_low, probs_low, ((0,), (0,)))
    normed = norm_ref[...]
    gain_part = (grad_normed * normed).astype(bf16)
    gain_cols = dot(gain_part, jnp.ones((rows, 128), bf16), ((0,), (0,)))
    if frames * H < head_lanes:
        lane = lax.broadcasted_iota(jnp.int32, (width, 128), 1)
        tail = head_lanes - 128
        if tail:
            cols_ref[:, :tail] = coefs[:, :tail].astype(bf16)
        cols_ref[:, tail:] = jnp.where(lane < frames * H - tail, coefs[:, tail:], gain_cols).astype(bf16)
    else:
        cols_ref[:, :head_lanes] = coefs.astype(bf16)
        cols_ref[:, head_lanes:] = gain_cols.astype(bf16)
    scaled = grad_normed * gain_ref[...]
    back = inv_ref[:, :1] * (
        scaled
        - jnp.mean(scaled, axis=1, keepdims=True)
        - normed * jnp.mean(scaled * normed, axis=1, keepdims=True)
    )
    for t in range(frames):
        gt_ref[t] = ((back[t * here : (t + 1) * here] + mix_ref[t : t + 1, :]) * patches).astype(bf16)


def final_kernel(
    frames, qk_ref, cols_ref, rows_ref,
    qkv_out, out_out, gloss_out, head_out, gain_out,
):
    clips, block, lanes = cols_ref.shape
    head_lanes = up(frames * H, 128)
    padded = rows_ref.shape[1]
    width, vocab = out_out.shape[1], gloss_out.shape[1]
    step = up(block, 128)

    def part(start, size):
        return rows_ref[:, :, start : start + size].astype(f32).reshape(clips * padded, size)

    at = 2 * width
    frame, att, head = [part(at + i * step, step)[:, :block] for i in range(3)]
    out_out[...] = dot(att.astype(bf16), part(0, width).astype(bf16), ((0,), (0,)))
    gloss_out[...] = dot(
        frame.astype(bf16), part(at + 3 * step, vocab).astype(bf16), ((0,), (0,))
    )
    head_out[...] = jnp.sum(head, axis=0, keepdims=True)
    gains = jnp.sum(cols_ref[:, :, lanes - 128 :].astype(f32), axis=0)
    gain_out[...] = jnp.transpose(gains)[127:128]
    values = None
    for c in range(clips):
        ga = by_head(rows_ref[c, :, width : 2 * width].astype(f32)[:frames], head_lanes).astype(bf16)
        part = dot(cols_ref[c, :, :head_lanes], ga)
        values = part if values is None else values + part
    low = low_lanes(block)
    for pair in range(H // 2):
        q = qk_ref[:, pair * 256 : pair * 256 + 128].astype(f32)
        k = qk_ref[:, pair * 256 + 128 : pair * 256 + 256].astype(f32)
        v = values[:, pair * 128 : (pair + 1) * 128]
        qkv_out[:, pair * 384 : pair * 384 + 128] = jnp.where(low, q, k)
        qkv_out[:, pair * 384 + 128 : pair * 384 + 256] = jnp.where(low, v, q)
        qkv_out[:, pair * 384 + 256 : pair * 384 + 384] = jnp.where(low, k, v)


def exchange_scratch(seq_count, clips, block, width, lanes, chunk_count):
    pairs, half = seq_count // 2, clips // 2
    wide = 2 * width + lanes
    piece = 2 * width // clips
    sems = pltpu.SemaphoreType.DMA
    return [
        pltpu.VMEM((pairs, block, wide), bf16),
        pltpu.VMEM((pairs, block, wide), bf16),
        pltpu.VMEM((pairs - 1, block, wide), bf16),
        pltpu.VMEM((block, wide), bf16),
        pltpu.VMEM((block, width), bf16),
        pltpu.VMEM((block, width), bf16),
        pltpu.VMEM((half - 1, block, piece), bf16),
        sems((2, seq_count - 1)),
        sems((2, half)),
        sems((2, chunk_count, 2 * pairs)),
        sems((2, chunk_count, pairs - 1)),
        sems((2, chunk_count)),
        sems((2, chunk_count, half - 1)),
        sems((2, chunk_count, half - 1)),
        sems((2, chunk_count, half - 1)),
        sems((2, chunk_count, 2)),
    ]


def exchange_kernel(
    chunk_count, dw_ref, cols_ref, rows_ref, gt_ref, sum_ref, all_cols_ref, all_rows_ref, back_ref,
    core_in, core_sum, pair_in, seq_sum, x_in, x_sum, z_in,
    token_sem, row_sem, core_sem, pair_sem, x_sem, z_sem, zq_sem, zc_sem, xg_sem,
):
    seq_count, local = back_ref.shape[:2]
    half = all_cols_ref.shape[1]
    pairs = seq_count // 2
    block, full = sum_ref.shape
    width = full // 2
    piece = width // half
    size = block // chunk_count
    me = lax.axis_index("seq")
    clip = lax.axis_index("clip")
    core, hi = lax.rem(me, 2), me // 2
    x, z = lax.rem(clip, 2), clip // 2

    def at(clip_id, seq_id):
        return (clip_id, seq_id)

    sibling = at(clip, hi * 2 + (1 - core))
    x_peer = at(z * 2 + (1 - x), me)

    def z_peer(step):
        return at(lax.rem(z + step, half) * 2 + x, me)

    barrier = pltpu.get_barrier_semaphore()
    peers = [at(clip, lax.rem(me + step, seq_count)) for step in range(1, seq_count)]
    peers += [x_peer] + [z_peer(step) for step in range(1, half)]
    for peer in peers:
        pl.semaphore_signal(barrier, inc=1, device_id=peer, device_id_type=pl.DeviceIdType.MESH)
    pl.semaphore_wait(barrier, len(peers))

    started = []

    def send(src, dst, sems, index, peer):
        copy = pltpu.make_async_remote_copy(
            src_ref=src,
            dst_ref=dst,
            send_sem=sems.at[(0,) + index],
            recv_sem=sems.at[(1,) + index],
            device_id=peer,
            device_id_type=pl.DeviceIdType.MESH,
        )
        copy.start()
        started.append(copy)
        return copy

    waits = {}

    def rows(c):
        return pl.ds(c * size, size)

    def block_rows(index, c):
        return pl.ds(pl.multiple_of(index * block + c * size, 16), size)

    def half_cols(index):
        return pl.ds(pl.multiple_of(index * width, 128), width)

    def first(c):
        waits[1, c] = []
        for p in range(pairs):
            src = block_rows(p * 2 + (1 - core), c)
            waits[1, c] += [
                send(dw_ref.at[src], core_in.at[p, rows(c), pl.ds(0, full)], core_sem, (c, 2 * p), sibling),
                send(
                    cols_ref.at[src],
                    core_in.at[p, rows(c), pl.ds(full, cols_ref.shape[1])],
                    core_sem,
                    (c, 2 * p + 1),
                    sibling,
                ),
            ]

    def second(c):
        for copy in waits[1, c]:
            copy.wait_recv()
        for p in range(pairs):
            own = block_rows(p * 2 + core, c)
            core_sum[p, rows(c), :full] = dw_ref[own, :] + core_in[p, rows(c), :full]
            core_sum[p, rows(c), full:] = cols_ref[own, :] + core_in[p, rows(c), full:]
        waits[2, c] = [
            send(
                core_sum.at[lax.rem(hi + step, pairs), rows(c)],
                pair_in.at[step - 1, rows(c)],
                pair_sem,
                (c, step - 1),
                at(clip, lax.rem(hi + step, pairs) * 2 + core),
            )
            for step in range(1, pairs)
        ]

    def third(c):
        for copy in waits[2, c]:
            copy.wait_recv()
        total = core_sum[hi, rows(c)].astype(f32)
        for step in range(pairs - 1):
            total += pair_in[step, rows(c)].astype(f32)
        total = total.astype(bf16)
        seq_sum[rows(c)] = total
        all_cols_ref[x, z, rows(c)] = total[:, full:]
        waits[3, c] = [
            send(seq_sum.at[rows(c), half_cols(1 - x)], x_in.at[rows(c)], x_sem, (c,), x_peer)
        ]
        waits[5, c] = [
            send(
                all_cols_ref.at[x, z, rows(c)],
                all_cols_ref.at[x, z, rows(c)],
                zc_sem,
                (c, step - 1),
                z_peer(step),
            )
            for step in range(1, half)
        ]

    def fourth(c):
        for copy in waits[3, c]:
            copy.wait_recv()
        x_sum[rows(c)] = seq_sum[rows(c), half_cols(x)] + x_in[rows(c)]
        waits[4, c] = [
            send(
                x_sum.at[rows(c), pl.ds(pl.multiple_of(lax.rem(z + step, half) * piece, 128), piece)],
                z_in.at[step - 1, rows(c)],
                z_sem,
                (c, step - 1),
                z_peer(step),
            )
            for step in range(1, half)
        ]

    def fifth(c):
        for copy in waits[4, c]:
            copy.wait_recv()
        total = x_sum[rows(c), pl.ds(pl.multiple_of(z * piece, 128), piece)].astype(f32)
        for step in range(half - 1):
            total += z_in[step, rows(c)].astype(f32)
        own = pl.ds(pl.multiple_of(x * width + z * piece, 128), piece)
        sum_ref[rows(c), own] = total.astype(bf16)
        waits[5, c] += [
            send(
                sum_ref.at[rows(c), own], sum_ref.at[rows(c), own], zq_sem, (c, step - 1), z_peer(step)
            )
            for step in range(1, half)
        ]

    def sixth(c):
        for copy in waits[5, c]:
            copy.wait_recv()
        mine = (rows(c), half_cols(x))
        waits[6, c] = [
            send(sum_ref.at[mine], sum_ref.at[mine], xg_sem, (c, 0), x_peer),
            send(
                all_cols_ref.at[x, :, rows(c)], all_cols_ref.at[x, :, rows(c)], xg_sem, (c, 1), x_peer
            ),
        ]

    def seventh(c):
        for copy in waits[6, c]:
            copy.wait_recv()

    stages = [first, second, third, fourth, fifth, sixth, seventh]
    for c in range(chunk_count):
        first(c)
    all_rows_ref[x, z] = rows_ref[...]
    row_waits = [
        send(rows_ref, all_rows_ref.at[x, z], row_sem, (step - 1,), z_peer(step))
        for step in range(1, half)
    ]
    token_waits = []
    for step in range(1, seq_count):
        to = lax.rem(me + step, seq_count)
        token_waits.append(
            send(gt_ref.at[pl.ds(to * local, local)], back_ref.at[me], token_sem, (step - 1,), at(clip, to))
        )
    back_ref[me] = gt_ref[pl.ds(me * local, local)]
    for wave in range(1, chunk_count + len(stages) - 1):
        for c in range(chunk_count):
            if 1 <= wave - c < len(stages):
                stages[wave - c](c)
        if wave == 2:
            for copy in row_waits:
                copy.wait_recv()
            row_waits = [send(all_rows_ref.at[x], all_rows_ref.at[x], row_sem, (half - 1,), x_peer)]
    for copy in row_waits + token_waits:
        copy.wait_recv()
    for copy in started:
        copy.wait_send()


def params():
    return pltpu.CompilerParams(vmem_limit_bytes=56 << 20)


def shape(dims, kind):
    return jax.ShapeDtypeStruct(dims, kind)


VM = pl.BlockSpec(memory_space=pltpu.VMEM)
SM = pl.BlockSpec(memory_space=pltpu.SMEM)


def per_device(
    clip_tokens, attn_gain, qkv_weight, out_weight, head_gain, gloss_weight, gloss_targets, target_lengths
):
    seq_count = lax.axis_size("seq")
    clips = lax.axis_size("clip")
    me = lax.axis_index("seq")
    local, patches, width = clip_tokens.shape[1:]
    vocab = gloss_weight.shape[1]
    frames = local * seq_count
    here = up(-(-patches // seq_count), 16)
    rows = frames * here
    head_lanes = up(frames * H, 128)
    lanes = up(frames * H + 1, 128)
    padded = up(frames, 8)
    block = width // seq_count
    gain_row = attn_gain.reshape(1, width)

    own = jnp.pad(clip_tokens[0], ((0, 0), (0, here * seq_count - patches), (0, 0)))
    q, k, v, probs, low, normed, inv, all_sums = pl.pallas_call(
        forward_kernel,
        out_shape=(
            shape((rows, width), bf16),
            shape((rows, width), bf16),
            shape((rows, width), bf16),
            shape((rows, head_lanes), f32),
            shape((rows, width), bf16),
            shape((rows, width), f32),
            shape((rows, 128), f32),
            shape((seq_count, 2, padded, width), f32),
        ),
        in_specs=[VM, VM, pl.BlockSpec(memory_space=pl.ANY)],
        out_specs=(VM,) * 8,
        scratch_shapes=[
            pltpu.VMEM((frames, here, width), bf16),
            pltpu.VMEM(qkv_weight.shape, bf16),
            pltpu.SemaphoreType.DMA,
            pltpu.SemaphoreType.DMA((2, seq_count - 1)),
            pltpu.SemaphoreType.DMA((2, seq_count - 1)),
        ],
        compiler_params=pltpu.CompilerParams(
            vmem_limit_bytes=56 << 20, collective_id=1, has_side_effects=True
        ),
        name="forward",
    )(own, gain_row, qkv_weight)
    loss, frame_rows, gl, head_part, grad_mixed, mixed_low, ga, sum_att = pl.pallas_call(
        functools.partial(middle_kernel, patches, frames),
        out_shape=(
            shape((8, 128), f32),
            shape((padded, width), bf16),
            shape((padded, vocab), bf16),
            shape((8, width), f32),
            shape((padded, width), f32),
            shape((padded, width), bf16),
            shape((padded, width), bf16),
            shape((padded, width), f32),
        ),
        in_specs=[SM, SM] + [VM] * 4,
        out_specs=(VM,) * 8,
        compiler_params=params(),
        name="middle",
    )(gloss_targets, target_lengths, all_sums, out_weight, head_gain.reshape(1, width), gloss_weight)

    def cut(array):
        part = lax.dynamic_slice_in_dim(array, me * block, block, 1)
        return jnp.pad(part.astype(bf16), ((0, 0), (0, up(block, 128) - block)))

    head8 = jnp.concatenate([head_part[:1], jnp.zeros((padded - 1, width), f32)], axis=0)
    packed = jnp.concatenate(
        [mixed_low, ga, cut(frame_rows), cut(sum_att), cut(head8), gl], axis=1
    )
    gt, dw, cols = pl.pallas_call(
        functools.partial(backward_kernel, patches, frames, here),
        out_shape=(
            shape((frames, here, width), bf16),
            shape((width, 2 * width), bf16),
            shape((width, lanes), bf16),
        ),
        in_specs=[VM] * 11,
        out_specs=(VM,) * 3,
        scratch_shapes=[pltpu.VMEM((rows, 2 * width), bf16)],
        compiler_params=params(),
        name="backward",
    )(q, k, v, probs, low, normed, inv, ga, grad_mixed, gain_row, qkv_weight)
    half = clips // 2
    chunk_count = min(8, block // 16)
    dw_sum, cols_all, gathered, back = pl.pallas_call(
        functools.partial(exchange_kernel, chunk_count),
        out_shape=(
            shape((block, 2 * width), bf16),
            shape((2, half, block, lanes), bf16),
            shape((2, half) + packed.shape, bf16),
            shape((seq_count, local, here, width), bf16),
        ),
        in_specs=[VM] * 4,
        out_specs=(VM,) * 4,
        scratch_shapes=exchange_scratch(seq_count, clips, block, width, lanes, chunk_count),
        compiler_params=pltpu.CompilerParams(
            vmem_limit_bytes=56 << 20, collective_id=0, has_side_effects=True
        ),
        name="exchange",
    )(dw, cols, packed, gt)
    cols_all = cols_all.reshape(clips, block, lanes)
    gathered = gathered.reshape((clips,) + packed.shape)
    back = back.transpose(1, 0, 2, 3).reshape(local, seq_count * here, width)
    grad_tokens = back[None, :, :patches]

    qkv_share, out_share, gloss_share, head_share, gain_share = pl.pallas_call(
        functools.partial(final_kernel, frames),
        out_shape=(
            shape((block, 3 * width), f32),
            shape((block, width), f32),
            shape((block, vocab), f32),
            shape((1, block), f32),
            shape((1, block), f32),
        ),
        in_specs=[VM] * 3,
        out_specs=(VM,) * 5,
        compiler_params=params(),
        name="final",
    )(dw_sum, cols_all, gathered)
    return (
        loss[0, :1],
        grad_tokens,
        gain_share[0],
        qkv_share,
        out_share,
        head_share[0],
        gloss_share,
    )


def solution(mesh):
    in_specs = (P("clip", "seq", None, None), P(), P(), P(), P(), P(), P("clip", None), P("clip"))
    out_specs = (
        P("clip"),
        P("clip", "seq", None, None),
        P("seq"),
        P("seq", None),
        P("seq", None),
        P("seq"),
        P("seq", None),
    )
    return jax.shard_map(
        per_device, mesh=mesh, in_specs=in_specs, out_specs=out_specs, check_vma=False
    )
```

```python
import functools

import jax
import jax.numpy as jnp
from jax import lax
from jax.experimental import pallas as pl
from jax.experimental.pallas import tpu as pltpu
from jax.sharding import PartitionSpec as P

H = 16
HD = 64
SCALE = HD ** (-0.5)

epsilon = 1e-06
very_low = -10000.0
f32 = jnp.float32
bf16 = jnp.bfloat16


def up(value, step):
    return -(-value // step) * step


def dot(left, right, dims=((1,), (0,))):
    return lax.dot_general(left, right, (dims, ((), ())), preferred_element_type=f32)


def spread(head_lanes, width, first, frame):
    row = lax.broadcasted_iota(jnp.int32, (head_lanes, width), 0)
    col = lax.broadcasted_iota(jnp.int32, (head_lanes, width), 1) + first
    return jnp.where(row == frame * H + lax.shift_right_logical(col, 6), 1.0, 0.0).astype(bf16)


def by_head(rows, head_lanes):
    count, width = rows.shape
    row = lax.broadcasted_iota(jnp.int32, (H, width), 0)
    col = lax.broadcasted_iota(jnp.int32, (H, width), 1)
    own = row == lax.shift_right_logical(col, 6)
    parts = [
        jnp.where(own, jnp.broadcast_to(rows[t : t + 1], (H, width)), 0.0) for t in range(count)
    ]
    if head_lanes > count * H:
        parts.append(jnp.zeros((head_lanes - count * H, width), f32))
    return jnp.concatenate(parts, axis=0)


def low_lanes(rows):
    return lax.broadcasted_iota(jnp.int32, (rows, 128), 1) < HD


def forward_kernel(
    own_ref, gain_ref, w_hbm, q_ref, k_ref, v_ref, p_ref, low_ref, norm_ref, inv_ref, all_sums_ref,
    x_ref, w_ref, w_sem, token_sem, sums_sem,
):
    frames, here, width = x_ref.shape
    local = own_ref.shape[0]
    seq_count = frames // local
    me = lax.axis_index("seq")
    clip = lax.axis_index("clip")
    w_copy = pltpu.make_async_copy(w_hbm, w_ref, w_sem)
    w_copy.start()
    barrier = pltpu.get_barrier_semaphore()
    for step in range(1, seq_count):
        pl.semaphore_signal(
            barrier,
            inc=1,
            device_id=(clip, lax.rem(me + step, seq_count)),
            device_id_type=pl.DeviceIdType.MESH,
        )
    pl.semaphore_wait(barrier, seq_count - 1)

    def send(src, dst, sems, step):
        copy = pltpu.make_async_remote_copy(
            src_ref=src,
            dst_ref=dst,
            send_sem=sems.at[0, step - 1],
            recv_sem=sems.at[1, step - 1],
            device_id=(clip, lax.rem(me + step, seq_count)),
            device_id_type=pl.DeviceIdType.MESH,
        )
        copy.start()
        return copy

    def patch_rows(device):
        return pl.ds(pl.multiple_of(device * here, 16), here)

    mine = pl.ds(me * local, local)
    tokens = [
        send(own_ref.at[:, patch_rows(lax.rem(me + step, seq_count))], x_ref.at[mine], token_sem, step)
        for step in range(1, seq_count)
    ]
    x_ref[mine] = own_ref[:, patch_rows(me)]
    for copy in tokens:
        copy.wait_recv()
    rows = frames * here
    head_lanes = p_ref.shape[1]
    x = x_ref[...].reshape(rows, width).astype(f32)
    centred = x - jnp.mean(x, axis=1, keepdims=True)
    inv = lax.rsqrt(jnp.mean(centred * centred, axis=1, keepdims=True) + epsilon)
    normed = centred * inv
    norm_ref[...] = normed
    inv_ref[...] = jnp.broadcast_to(inv, (rows, 128))
    low_ref[...] = (normed * gain_ref[...]).astype(bf16)
    low = low_lanes(rows)
    w_copy.wait()
    for pair in range(H // 2):
        y = dot(low_ref[...], w_ref[:, pair * 384 : (pair + 1) * 384])
        a, b, c = y[:, :128], y[:, 128:256], y[:, 256:]
        at = slice(pair * 128, (pair + 1) * 128)
        q_ref[:, at] = jnp.where(low, a, b).astype(bf16)
        k_ref[:, at] = pltpu.roll(jnp.where(low, c, a), HD, 1).astype(bf16)
        v_ref[:, at] = jnp.where(low, b, c).astype(bf16)
    keys = k_ref[...].astype(f32).reshape(frames, here, width)
    scores = jnp.zeros((rows, head_lanes), f32)
    for t in range(frames):
        q_t = q_ref[t * here : (t + 1) * here, :].astype(f32)
        prod = (keys * q_t[None]).reshape(rows, width).astype(bf16)
        scores += dot(prod, spread(head_lanes, width, 0, t), ((1,), (1,)))
    raised = jnp.exp(scores * SCALE).reshape(frames, here, head_lanes)
    probs = raised / jnp.sum(raised, axis=0, keepdims=True)
    probs = probs.reshape(rows, head_lanes)
    p_ref[...] = probs
    mixed = dot(probs.astype(bf16), v_ref[...], ((0,), (0,)))
    row = lax.broadcasted_iota(jnp.int32, (H, width), 0)
    col = lax.broadcasted_iota(jnp.int32, (H, width), 1)
    own = row == lax.shift_right_logical(col, 6)
    padded = all_sums_ref.shape[2]
    blank = [jnp.zeros((padded - frames, width), f32)] if padded > frames else []
    tok = [jnp.sum(x[t * here : (t + 1) * here], axis=0, keepdims=True) for t in range(frames)]
    att = [
        jnp.sum(jnp.where(own, mixed[t * H : (t + 1) * H], 0.0), axis=0, keepdims=True)
        for t in range(frames)
    ]
    all_sums_ref[me, 0] = jnp.concatenate(tok + blank, axis=0)
    all_sums_ref[me, 1] = jnp.concatenate(att + blank, axis=0)
    sums = [send(all_sums_ref.at[me], all_sums_ref.at[me], sums_sem, step) for step in range(1, seq_count)]
    for copy in sums:
        copy.wait_recv()
    for copy in tokens + sums:
        copy.wait_send()


def add_log(left, right):
    top = jnp.maximum(left, right)
    return top + jnp.log(1.0 + jnp.exp(-jnp.abs(left - right)))


def middle_kernel(
    patches, frames, labels_ref, length_ref, sums_ref, wo_ref, gain_ref, wg_ref,
    loss_ref, packed_ref, mix_ref, ga_ref, wide_ref,
):
    width = wo_ref.shape[0]
    block = width // sums_ref.shape[0]
    step = up(block, 128)
    total = jnp.sum(sums_ref[...], axis=0)
    sum_tok, sum_att = total[0], total[1]
    wide_ref[1] = sum_att
    hi = sum_att.astype(bf16)
    lo = (sum_att - hi.astype(f32)).astype(bf16)
    pooled = (sum_tok + dot(hi, wo_ref[...]) + dot(lo, wo_ref[...])) * (1.0 / patches)
    centred = pooled - jnp.mean(pooled, axis=1, keepdims=True)
    inv = lax.rsqrt(jnp.mean(centred * centred, axis=1, keepdims=True) + epsilon)
    plain = centred * inv
    frame = (plain * gain_ref[...]).astype(bf16)
    wide_ref[0] = frame.astype(f32)
    logits = dot(frame, wg_ref[...], ((1,), (1,)))
    padded, vocab = logits.shape
    raised = jnp.exp(logits)
    denom = jnp.sum(raised, axis=1, keepdims=True)
    soft = raised / denom
    logs = logits - jnp.log(denom)
    cap = labels_ref.shape[1]
    length = length_ref[0]
    lane = lax.broadcasted_iota(jnp.int32, (1, 128), 1)
    gloss = lax.broadcasted_iota(jnp.int32, (padded, vocab), 1)

    def pick(label):
        return jnp.sum(jnp.where(gloss == label, logs, 0.0), axis=1, keepdims=True)

    wide = lax.broadcasted_iota(jnp.int32, (padded, 128), 1)
    emitted = jnp.where((wide & 1) == 0, pick(0), 0.0)
    skip = lane < 0
    for i in range(cap):
        label = labels_ref[0, i]
        emitted = jnp.where(wide == 2 * i + 1, pick(label), emitted)
        before = labels_ref[0, i - 1] if i else -1
        skip = skip | ((lane == 2 * i + 1) & (label != before))
    usable = lane < 2 * length + 1
    start = (lane < 2) & usable
    alphas = jnp.where(start, emitted[0:1], very_low)
    kept = []
    for t in range(1, frames):
        one = jnp.where(lane < 1, very_low, pltpu.roll(alphas, 1, 1))
        two = jnp.where(skip, pltpu.roll(alphas, 2, 1), very_low)
        outer = add_log(add_log(alphas, one), two)
        kept.append((jnp.exp(alphas - outer), jnp.exp(one - outer), jnp.exp(two - outer)))
        alphas = jnp.where(usable, outer + emitted[t : t + 1], very_low)
    last = jnp.sum(jnp.where(lane == 2 * length, alphas, 0.0), axis=1, keepdims=True)
    prior = jnp.sum(jnp.where(lane == 2 * length - 1, alphas, 0.0), axis=1, keepdims=True)
    ending = add_log(last, prior)
    share = 1.0 / length.astype(f32)
    loss_ref[...] = jnp.broadcast_to(-ending * share, (8, 128))
    grad = jnp.where(
        (lane == 2 * length) | (lane == 2 * length - 1), -share * jnp.exp(alphas - ending), 0.0
    )
    row = lax.broadcasted_iota(jnp.int32, (padded, 128), 0)
    emit_grad = jnp.zeros((padded, 128), f32)
    for t in range(frames - 1, 0, -1):
        grad = jnp.where(usable, grad, 0.0)
        emit_grad = jnp.where(row == t, grad, emit_grad)
        w_own, w_one, w_two = kept[t - 1]
        from_one = jnp.where(lane < 1, 0.0, grad * w_one)
        from_two = jnp.where(skip, grad * w_two, 0.0)
        from_two = jnp.where(lane < 2, 0.0, from_two)
        grad = grad * w_own + pltpu.roll(from_one, 127, 1) + pltpu.roll(from_two, 126, 1)
    emit_grad = jnp.where(row == 0, jnp.where(start, grad, 0.0), emit_grad)
    blank = jnp.sum(jnp.where((wide & 1) == 0, emit_grad, 0.0), axis=1, keepdims=True)
    d_logs = jnp.where(gloss == 0, blank, 0.0)
    for i in range(cap):
        part = jnp.sum(jnp.where(wide == 2 * i + 1, emit_grad, 0.0), axis=1, keepdims=True)
        d_logs = d_logs + jnp.where(gloss == labels_ref[0, i], part, 0.0)
    d_logits = d_logs - soft * jnp.sum(emit_grad, axis=1, keepdims=True)
    gl = d_logits.astype(bf16)
    packed_ref[:, 2 * width + 3 * step :] = gl
    grad_frame = dot(gl, wg_ref[...])
    head = jnp.sum(grad_frame * plain, axis=0, keepdims=True)
    first_row = lax.broadcasted_iota(jnp.int32, (padded, width), 0) == 0
    wide_ref[2] = jnp.where(first_row, jnp.broadcast_to(head, (padded, width)), 0.0)
    start_at = lax.axis_index("seq") * block
    for i in range(3):
        part = wide_ref[i, :, pl.ds(pl.multiple_of(start_at // 128 * 128, 128), step)]
        for shift in range(block, 128, block):
            part = jnp.where(lax.rem(start_at, 128) == shift, pltpu.roll(part, 128 - shift, 1), part)
        packed_ref[:, 2 * width + i * step : 2 * width + (i + 1) * step] = part.astype(bf16)
    scaled = grad_frame * gain_ref[...]
    grad_pooled = inv * (
        scaled
        - jnp.mean(scaled, axis=1, keepdims=True)
        - plain * jnp.mean(scaled * plain, axis=1, keepdims=True)
    )
    grad_mixed = grad_pooled * (1.0 / patches)
    mix_ref[...] = grad_mixed
    mixed_low = grad_mixed.astype(bf16)
    packed_ref[:, :width] = mixed_low
    ga = dot(mixed_low, wo_ref[...], ((1,), (1,))).astype(bf16)
    ga_ref[...] = ga
    packed_ref[:, width : 2 * width] = ga


def backward_kernel(
    patches, frames, here, q_ref, k_ref, v_ref, p_ref, low_ref, norm_ref, inv_ref, ga_ref, mix_ref,
    gain_ref, w_ref, gt_ref, dw_ref, cols_ref, qk_ref,
):
    rows, width = q_ref.shape
    head_lanes = p_ref.shape[1]
    ga = by_head(ga_ref[...].astype(f32)[:frames], head_lanes).astype(bf16)
    probs = p_ref[...]
    probs_low = probs.astype(bf16)
    grad_probs = dot(v_ref[...], ga, ((1,), (1,)))
    inner = jnp.sum((grad_probs * probs).reshape(frames, here, head_lanes), axis=0, keepdims=True)
    grad_scores = probs.reshape(frames, here, head_lanes) * (
        grad_probs.reshape(frames, here, head_lanes) - inner
    )
    scores_low = (grad_scores.reshape(rows, head_lanes) * SCALE).astype(bf16)
    low = low_lanes(rows)
    for pair in range(H // 2):
        at = slice(pair * 128, (pair + 1) * 128)
        keys = k_ref[:, at].astype(f32).reshape(frames, here, 128)
        grad_keys = jnp.zeros((frames, here, 128), f32)
        queries = []
        for t in range(frames):
            wide = dot(scores_low, spread(head_lanes, 128, pair * 128, t)).reshape(frames, here, 128)
            queries.append(jnp.sum(wide * keys, axis=0))
            q_t = q_ref[t * here : (t + 1) * here, at].astype(f32)
            grad_keys += wide * q_t[None]
        gq = jnp.concatenate(queries, axis=0)
        gk = pltpu.roll(grad_keys.reshape(rows, 128), HD, 1)
        gv = dot(probs_low, ga[:, at])
        qk_ref[:, pair * 256 : pair * 256 + 128] = gq.astype(bf16)
        qk_ref[:, pair * 256 + 128 : pair * 256 + 256] = gk.astype(bf16)
        a = jnp.where(low, gq, gk).astype(bf16)
        b = jnp.where(low, gv, gq).astype(bf16)
        c = jnp.where(low, gk, gv).astype(bf16)
        part = dot(
            jnp.concatenate([a, b, c], axis=1), w_ref[:, pair * 384 : (pair + 1) * 384], ((1,), (1,))
        )
        if pair == 0:
            grad_normed = part
        else:
            grad_normed += part
    tokens_low = low_ref[...]
    chunk = 512
    for start in range(0, 2 * width, chunk):
        dw_ref[:, start : start + chunk] = dot(
            tokens_low, qk_ref[:, start : start + chunk], ((0,), (0,))
        ).astype(bf16)
    coefs = dot(tokens_low, probs_low, ((0,), (0,)))
    normed = norm_ref[...]
    gain_part = (grad_normed * normed).astype(bf16)
    gain_cols = dot(gain_part, jnp.ones((rows, 128), bf16), ((0,), (0,)))
    if frames * H < head_lanes:
        lane = lax.broadcasted_iota(jnp.int32, (width, 128), 1)
        tail = head_lanes - 128
        if tail:
            cols_ref[:, :tail] = coefs[:, :tail].astype(bf16)
        cols_ref[:, tail:] = jnp.where(lane < frames * H - tail, coefs[:, tail:], gain_cols).astype(bf16)
    else:
        cols_ref[:, :head_lanes] = coefs.astype(bf16)
        cols_ref[:, head_lanes:] = gain_cols.astype(bf16)
    scaled = grad_normed * gain_ref[...]
    back = inv_ref[:, :1] * (
        scaled
        - jnp.mean(scaled, axis=1, keepdims=True)
        - normed * jnp.mean(scaled * normed, axis=1, keepdims=True)
    )
    for t in range(frames):
        gt_ref[t] = ((back[t * here : (t + 1) * here] + mix_ref[t : t + 1, :]) * patches).astype(bf16)


def final_kernel(
    frames, qk_ref, cols_ref, rows_ref,
    qkv_out, out_out, gloss_out, head_out, gain_out,
):
    clips, block, lanes = cols_ref.shape
    head_lanes = up(frames * H, 128)
    padded = rows_ref.shape[1]
    width, vocab = out_out.shape[1], gloss_out.shape[0]
    step = up(block, 128)

    def part(start, size):
        return rows_ref[:, :, start : start + size].astype(f32).reshape(clips * padded, size)

    at = 2 * width
    frame, att, head = [part(at + i * step, step)[:, :block] for i in range(3)]
    out_out[...] = dot(att.astype(bf16), part(0, width).astype(bf16), ((0,), (0,)))
    gloss_out[...] = dot(
        part(at + 3 * step, vocab).astype(bf16), frame.astype(bf16), ((0,), (0,))
    )
    head_out[...] = jnp.sum(head, axis=0, keepdims=True)
    gains = jnp.sum(cols_ref[:, :, lanes - 128 :].astype(f32), axis=0)
    gain_out[...] = jnp.transpose(gains)[127:128]
    values = None
    for c in range(clips):
        ga = by_head(rows_ref[c, :, width : 2 * width].astype(f32)[:frames], head_lanes).astype(bf16)
        part = dot(cols_ref[c, :, :head_lanes], ga)
        values = part if values is None else values + part
    low = low_lanes(block)
    for pair in range(H // 2):
        q = qk_ref[:, pair * 256 : pair * 256 + 128].astype(f32)
        k = qk_ref[:, pair * 256 + 128 : pair * 256 + 256].astype(f32)
        v = values[:, pair * 128 : (pair + 1) * 128]
        qkv_out[:, pair * 384 : pair * 384 + 128] = jnp.where(low, q, k)
        qkv_out[:, pair * 384 + 128 : pair * 384 + 256] = jnp.where(low, v, q)
        qkv_out[:, pair * 384 + 256 : pair * 384 + 384] = jnp.where(low, k, v)


def exchange_scratch(seq_count, clips, block, width, lanes, chunk_count):
    pairs, half = seq_count // 2, clips // 2
    wide = 2 * width + lanes
    piece = 2 * width // clips
    sems = pltpu.SemaphoreType.DMA
    return [
        pltpu.VMEM((pairs, block, wide), bf16),
        pltpu.VMEM((pairs, block, wide), bf16),
        pltpu.VMEM((pairs - 1, block, wide), bf16),
        pltpu.VMEM((block, wide), bf16),
        pltpu.VMEM((block, width), bf16),
        pltpu.VMEM((block, width), bf16),
        pltpu.VMEM((half - 1, block, piece), bf16),
        sems((2, seq_count - 1)),
        sems((2, half)),
        sems((2, chunk_count, 2 * pairs)),
        sems((2, chunk_count, pairs - 1)),
        sems((2, chunk_count)),
        sems((2, chunk_count, half - 1)),
        sems((2, chunk_count, half - 1)),
        sems((2, chunk_count, half - 1)),
        sems((2, chunk_count, 2)),
    ]


def exchange_kernel(
    chunk_count, dw_ref, cols_ref, rows_ref, gt_ref, sum_ref, all_cols_ref, all_rows_ref, back_ref,
    core_in, core_sum, pair_in, seq_sum, x_in, x_sum, z_in,
    token_sem, row_sem, core_sem, pair_sem, x_sem, z_sem, zq_sem, zc_sem, xg_sem,
):
    seq_count, local = back_ref.shape[:2]
    half = all_cols_ref.shape[1]
    pairs = seq_count // 2
    block, full = sum_ref.shape
    width = full // 2
    piece = width // half
    size = block // chunk_count
    me = lax.axis_index("seq")
    clip = lax.axis_index("clip")
    core, hi = lax.rem(me, 2), me // 2
    x, z = lax.rem(clip, 2), clip // 2

    def at(clip_id, seq_id):
        return (clip_id, seq_id)

    sibling = at(clip, hi * 2 + (1 - core))
    x_peer = at(z * 2 + (1 - x), me)

    def z_peer(step):
        return at(lax.rem(z + step, half) * 2 + x, me)

    barrier = pltpu.get_barrier_semaphore()
    peers = [at(clip, lax.rem(me + step, seq_count)) for step in range(1, seq_count)]
    peers += [x_peer] + [z_peer(step) for step in range(1, half)]
    for peer in peers:
        pl.semaphore_signal(barrier, inc=1, device_id=peer, device_id_type=pl.DeviceIdType.MESH)
    pl.semaphore_wait(barrier, len(peers))

    started = []

    def send(src, dst, sems, index, peer):
        copy = pltpu.make_async_remote_copy(
            src_ref=src,
            dst_ref=dst,
            send_sem=sems.at[(0,) + index],
            recv_sem=sems.at[(1,) + index],
            device_id=peer,
            device_id_type=pl.DeviceIdType.MESH,
        )
        copy.start()
        started.append(copy)
        return copy

    waits = {}

    def rows(c):
        return pl.ds(c * size, size)

    def block_rows(index, c):
        return pl.ds(pl.multiple_of(index * block + c * size, 16), size)

    def half_cols(index):
        return pl.ds(pl.multiple_of(index * width, 128), width)

    def first(c):
        waits[1, c] = []
        for p in range(pairs):
            src = block_rows(p * 2 + (1 - core), c)
            waits[1, c] += [
                send(dw_ref.at[src], core_in.at[p, rows(c), pl.ds(0, full)], core_sem, (c, 2 * p), sibling),
                send(
                    cols_ref.at[src],
                    core_in.at[p, rows(c), pl.ds(full, cols_ref.shape[1])],
                    core_sem,
                    (c, 2 * p + 1),
                    sibling,
                ),
            ]

    def second(c):
        for copy in waits[1, c]:
            copy.wait_recv()
        for p in range(pairs):
            own = block_rows(p * 2 + core, c)
            core_sum[p, rows(c), :full] = dw_ref[own, :] + core_in[p, rows(c), :full]
            core_sum[p, rows(c), full:] = cols_ref[own, :] + core_in[p, rows(c), full:]
        waits[2, c] = [
            send(
                core_sum.at[lax.rem(hi + step, pairs), rows(c)],
                pair_in.at[step - 1, rows(c)],
                pair_sem,
                (c, step - 1),
                at(clip, lax.rem(hi + step, pairs) * 2 + core),
            )
            for step in range(1, pairs)
        ]

    def third(c):
        for copy in waits[2, c]:
            copy.wait_recv()
        total = core_sum[hi, rows(c)].astype(f32)
        for step in range(pairs - 1):
            total += pair_in[step, rows(c)].astype(f32)
        total = total.astype(bf16)
        seq_sum[rows(c)] = total
        all_cols_ref[x, z, rows(c)] = total[:, full:]
        waits[3, c] = [
            send(seq_sum.at[rows(c), half_cols(1 - x)], x_in.at[rows(c)], x_sem, (c,), x_peer)
        ]
        waits[5, c] = [
            send(
                all_cols_ref.at[x, z, rows(c)],
                all_cols_ref.at[x, z, rows(c)],
                zc_sem,
                (c, step - 1),
                z_peer(step),
            )
            for step in range(1, half)
        ]

    def fourth(c):
        for copy in waits[3, c]:
            copy.wait_recv()
        x_sum[rows(c)] = seq_sum[rows(c), half_cols(x)] + x_in[rows(c)]
        waits[4, c] = [
            send(
                x_sum.at[rows(c), pl.ds(pl.multiple_of(lax.rem(z + step, half) * piece, 128), piece)],
                z_in.at[step - 1, rows(c)],
                z_sem,
                (c, step - 1),
                z_peer(step),
            )
            for step in range(1, half)
        ]

    def fifth(c):
        for copy in waits[4, c]:
            copy.wait_recv()
        total = x_sum[rows(c), pl.ds(pl.multiple_of(z * piece, 128), piece)].astype(f32)
        for step in range(half - 1):
            total += z_in[step, rows(c)].astype(f32)
        own = pl.ds(pl.multiple_of(x * width + z * piece, 128), piece)
        sum_ref[rows(c), own] = total.astype(bf16)
        waits[5, c] += [
            send(
                sum_ref.at[rows(c), own], sum_ref.at[rows(c), own], zq_sem, (c, step - 1), z_peer(step)
            )
            for step in range(1, half)
        ]

    def sixth(c):
        for copy in waits[5, c]:
            copy.wait_recv()
        mine = (rows(c), half_cols(x))
        waits[6, c] = [
            send(sum_ref.at[mine], sum_ref.at[mine], xg_sem, (c, 0), x_peer),
            send(
                all_cols_ref.at[x, :, rows(c)], all_cols_ref.at[x, :, rows(c)], xg_sem, (c, 1), x_peer
            ),
        ]

    def seventh(c):
        for copy in waits[6, c]:
            copy.wait_recv()

    stages = [first, second, third, fourth, fifth, sixth, seventh]
    for c in range(chunk_count):
        first(c)
    all_rows_ref[x, z] = rows_ref[...]
    row_waits = [
        send(rows_ref, all_rows_ref.at[x, z], row_sem, (step - 1,), z_peer(step))
        for step in range(1, half)
    ]
    token_waits = []
    for step in range(1, seq_count):
        to = lax.rem(me + step, seq_count)
        token_waits.append(
            send(gt_ref.at[pl.ds(to * local, local)], back_ref.at[me], token_sem, (step - 1,), at(clip, to))
        )
    back_ref[me] = gt_ref[pl.ds(me * local, local)]
    for wave in range(1, chunk_count + len(stages) - 1):
        for c in range(chunk_count):
            if 1 <= wave - c < len(stages):
                stages[wave - c](c)
        if wave == 2:
            for copy in row_waits:
                copy.wait_recv()
            row_waits = [send(all_rows_ref.at[x], all_rows_ref.at[x], row_sem, (half - 1,), x_peer)]
    for copy in row_waits + token_waits:
        copy.wait_recv()
    for copy in started:
        copy.wait_send()


def params():
    return pltpu.CompilerParams(vmem_limit_bytes=56 << 20)


def shape(dims, kind):
    return jax.ShapeDtypeStruct(dims, kind)


VM = pl.BlockSpec(memory_space=pltpu.VMEM)
SM = pl.BlockSpec(memory_space=pltpu.SMEM)


def per_device(
    clip_tokens, attn_gain, qkv_weight, out_weight, head_gain, gloss_weight, gloss_targets, target_lengths
):
    seq_count = lax.axis_size("seq")
    clips = lax.axis_size("clip")
    me = lax.axis_index("seq")
    local, patches, width = clip_tokens.shape[1:]
    vocab = gloss_weight.shape[1]
    frames = local * seq_count
    here = up(-(-patches // seq_count), 16)
    rows = frames * here
    head_lanes = up(frames * H, 128)
    lanes = up(frames * H + 1, 128)
    padded = up(frames, 8)
    block = width // seq_count
    gain_row = attn_gain.reshape(1, width)

    own = jnp.pad(clip_tokens[0], ((0, 0), (0, here * seq_count - patches), (0, 0)))
    q, k, v, probs, low, normed, inv, all_sums = pl.pallas_call(
        forward_kernel,
        out_shape=(
            shape((rows, width), bf16),
            shape((rows, width), bf16),
            shape((rows, width), bf16),
            shape((rows, head_lanes), f32),
            shape((rows, width), bf16),
            shape((rows, width), f32),
            shape((rows, 128), f32),
            shape((seq_count, 2, padded, width), f32),
        ),
        in_specs=[VM, VM, pl.BlockSpec(memory_space=pl.ANY)],
        out_specs=(VM,) * 8,
        scratch_shapes=[
            pltpu.VMEM((frames, here, width), bf16),
            pltpu.VMEM(qkv_weight.shape, bf16),
            pltpu.SemaphoreType.DMA,
            pltpu.SemaphoreType.DMA((2, seq_count - 1)),
            pltpu.SemaphoreType.DMA((2, seq_count - 1)),
        ],
        compiler_params=pltpu.CompilerParams(
            vmem_limit_bytes=56 << 20, collective_id=1, has_side_effects=True
        ),
        name="forward",
    )(own, gain_row, qkv_weight)
    loss, packed, grad_mixed, ga = pl.pallas_call(
        functools.partial(middle_kernel, patches, frames),
        out_shape=(
            shape((8, 128), f32),
            shape((padded, 2 * width + 3 * up(block, 128) + vocab), bf16),
            shape((padded, width), f32),
            shape((padded, width), bf16),
        ),
        in_specs=[SM, SM] + [VM] * 4,
        out_specs=(VM,) * 4,
        scratch_shapes=[pltpu.VMEM((3, padded, width), f32)],
        compiler_params=params(),
        name="middle",
    )(gloss_targets, target_lengths, all_sums, out_weight, head_gain.reshape(1, width), gloss_weight.T)

    gt, dw, cols = pl.pallas_call(
        functools.partial(backward_kernel, patches, frames, here),
        out_shape=(
            shape((frames, here, width), bf16),
            shape((width, 2 * width), bf16),
            shape((width, lanes), bf16),
        ),
        in_specs=[VM] * 11,
        out_specs=(VM,) * 3,
        scratch_shapes=[pltpu.VMEM((rows, 2 * width), bf16)],
        compiler_params=params(),
        name="backward",
    )(q, k, v, probs, low, normed, inv, ga, grad_mixed, gain_row, qkv_weight)
    half = clips // 2
    chunk_count = 4
    dw_sum, cols_all, gathered, back = pl.pallas_call(
        functools.partial(exchange_kernel, chunk_count),
        out_shape=(
            shape((block, 2 * width), bf16),
            shape((2, half, block, lanes), bf16),
            shape((2, half) + packed.shape, bf16),
            shape((seq_count, local, here, width), bf16),
        ),
        in_specs=[VM] * 4,
        out_specs=(VM,) * 4,
        scratch_shapes=exchange_scratch(seq_count, clips, block, width, lanes, chunk_count),
        compiler_params=pltpu.CompilerParams(
            vmem_limit_bytes=56 << 20, collective_id=0, has_side_effects=True
        ),
        name="exchange",
    )(dw, cols, packed, gt)
    cols_all = cols_all.reshape(clips, block, lanes)
    gathered = gathered.reshape((clips,) + packed.shape)
    back = back.transpose(1, 0, 2, 3).reshape(local, seq_count * here, width)
    grad_tokens = back[None, :, :patches]

    qkv_share, out_share, gloss_share, head_share, gain_share = pl.pallas_call(
        functools.partial(final_kernel, frames),
        out_shape=(
            shape((block, 3 * width), f32),
            shape((block, width), f32),
            shape((vocab, block), f32),
            shape((1, block), f32),
            shape((1, block), f32),
        ),
        in_specs=[VM] * 3,
        out_specs=(VM,) * 5,
        compiler_params=params(),
        name="final",
    )(dw_sum, cols_all, gathered)
    return (
        loss[0, :1],
        grad_tokens,
        gain_share[0],
        qkv_share,
        out_share,
        head_share[0],
        gloss_share.T,
    )


def solution(mesh):
    in_specs = (P("clip", "seq", None, None), P(), P(), P(), P(), P(), P("clip", None), P("clip"))
    out_specs = (
        P("clip"),
        P("clip", "seq", None, None),
        P("seq"),
        P("seq", None),
        P("seq", None),
        P("seq"),
        P("seq", None),
    )
    return jax.shard_map(
        per_device, mesh=mesh, in_specs=in_specs, out_specs=out_specs, check_vma=False
    )
```

```python
import functools

import jax
import jax.numpy as jnp
from jax import lax
from jax.experimental import pallas as pl
from jax.experimental.pallas import tpu as pltpu
from jax.sharding import PartitionSpec as P

H = 16
HD = 64
SCALE = HD ** (-0.5)

epsilon = 1e-06
very_low = -10000.0
f32 = jnp.float32
bf16 = jnp.bfloat16


def up(value, step):
    return -(-value // step) * step


def dot(left, right, dims=((1,), (0,))):
    return lax.dot_general(left, right, (dims, ((), ())), preferred_element_type=f32)


def spread(head_lanes, width, first, frame):
    row = lax.broadcasted_iota(jnp.int32, (head_lanes, width), 0)
    col = lax.broadcasted_iota(jnp.int32, (head_lanes, width), 1) + first
    return jnp.where(row == frame * H + lax.shift_right_logical(col, 6), 1.0, 0.0).astype(bf16)


def by_head(rows, head_lanes):
    count, width = rows.shape
    row = lax.broadcasted_iota(jnp.int32, (H, width), 0)
    col = lax.broadcasted_iota(jnp.int32, (H, width), 1)
    own = row == lax.shift_right_logical(col, 6)
    parts = [
        jnp.where(own, jnp.broadcast_to(rows[t : t + 1], (H, width)), 0.0) for t in range(count)
    ]
    if head_lanes > count * H:
        parts.append(jnp.zeros((head_lanes - count * H, width), f32))
    return jnp.concatenate(parts, axis=0)


def low_lanes(rows):
    return lax.broadcasted_iota(jnp.int32, (rows, 128), 1) < HD


def forward_kernel(
    own_ref, gain_ref, w_hbm, q_ref, k_ref, v_ref, p_ref, low_ref, norm_ref, inv_ref, all_sums_ref,
    x_ref, w_ref, w_sem, token_sem, sums_sem,
):
    frames, here, width = x_ref.shape
    local = own_ref.shape[0]
    seq_count = frames // local
    me = lax.axis_index("seq")
    clip = lax.axis_index("clip")
    w_copy = pltpu.make_async_copy(w_hbm, w_ref, w_sem)
    w_copy.start()
    barrier = pltpu.get_barrier_semaphore()
    for step in range(1, seq_count):
        pl.semaphore_signal(
            barrier,
            inc=1,
            device_id=(clip, lax.rem(me + step, seq_count)),
            device_id_type=pl.DeviceIdType.MESH,
        )
    pl.semaphore_wait(barrier, seq_count - 1)

    def send(src, dst, sems, step):
        copy = pltpu.make_async_remote_copy(
            src_ref=src,
            dst_ref=dst,
            send_sem=sems.at[0, step - 1],
            recv_sem=sems.at[1, step - 1],
            device_id=(clip, lax.rem(me + step, seq_count)),
            device_id_type=pl.DeviceIdType.MESH,
        )
        copy.start()
        return copy

    def patch_rows(device):
        return pl.ds(pl.multiple_of(device * here, 16), here)

    mine = pl.ds(me * local, local)
    tokens = [
        send(own_ref.at[:, patch_rows(lax.rem(me + step, seq_count))], x_ref.at[mine], token_sem, step)
        for step in range(1, seq_count)
    ]
    x_ref[mine] = own_ref[:, patch_rows(me)]
    for copy in tokens:
        copy.wait_recv()
    rows = frames * here
    head_lanes = p_ref.shape[1]
    x = x_ref[...].reshape(rows, width).astype(f32)
    centred = x - jnp.mean(x, axis=1, keepdims=True)
    inv = lax.rsqrt(jnp.mean(centred * centred, axis=1, keepdims=True) + epsilon)
    normed = centred * inv
    norm_ref[...] = normed
    inv_ref[...] = jnp.broadcast_to(inv, (rows, 128))
    low_ref[...] = (normed * gain_ref[...]).astype(bf16)
    low = low_lanes(rows)
    w_copy.wait()
    for pair in range(H // 2):
        y = dot(low_ref[...], w_ref[:, pair * 384 : (pair + 1) * 384])
        a, b, c = y[:, :128], y[:, 128:256], y[:, 256:]
        at = slice(pair * 128, (pair + 1) * 128)
        q_ref[:, at] = jnp.where(low, a, b).astype(bf16)
        k_ref[:, at] = pltpu.roll(jnp.where(low, c, a), HD, 1).astype(bf16)
        v_ref[:, at] = jnp.where(low, b, c).astype(bf16)
    keys = k_ref[...].astype(f32).reshape(frames, here, width)
    scores = jnp.zeros((rows, head_lanes), f32)
    for t in range(frames):
        q_t = q_ref[t * here : (t + 1) * here, :].astype(f32)
        prod = (keys * q_t[None]).reshape(rows, width).astype(bf16)
        scores += dot(prod, spread(head_lanes, width, 0, t), ((1,), (1,)))
    raised = jnp.exp(scores * SCALE).reshape(frames, here, head_lanes)
    probs = raised / jnp.sum(raised, axis=0, keepdims=True)
    probs = probs.reshape(rows, head_lanes)
    p_ref[...] = probs
    mixed = dot(probs.astype(bf16), v_ref[...], ((0,), (0,)))
    row = lax.broadcasted_iota(jnp.int32, (H, width), 0)
    col = lax.broadcasted_iota(jnp.int32, (H, width), 1)
    own = row == lax.shift_right_logical(col, 6)
    padded = all_sums_ref.shape[2]
    blank = [jnp.zeros((padded - frames, width), f32)] if padded > frames else []
    tok = [jnp.sum(x[t * here : (t + 1) * here], axis=0, keepdims=True) for t in range(frames)]
    att = [
        jnp.sum(jnp.where(own, mixed[t * H : (t + 1) * H], 0.0), axis=0, keepdims=True)
        for t in range(frames)
    ]
    all_sums_ref[me, 0] = jnp.concatenate(tok + blank, axis=0)
    all_sums_ref[me, 1] = jnp.concatenate(att + blank, axis=0)
    sums = [send(all_sums_ref.at[me], all_sums_ref.at[me], sums_sem, step) for step in range(1, seq_count)]
    for copy in sums:
        copy.wait_recv()
    for copy in tokens + sums:
        copy.wait_send()


def add_log(left, right):
    top = jnp.maximum(left, right)
    return top + jnp.log(1.0 + jnp.exp(-jnp.abs(left - right)))


def middle_kernel(
    patches, frames, labels_ref, length_ref, sums_ref, wo_ref, gain_ref, wg_ref,
    loss_ref, packed_ref, mix_ref, ga_ref, wide_ref,
):
    width = wo_ref.shape[0]
    block = width // sums_ref.shape[0]
    step = up(block, 128)
    total = jnp.sum(sums_ref[...], axis=0)
    sum_tok, sum_att = total[0], total[1]
    wide_ref[1] = sum_att
    hi = sum_att.astype(bf16)
    lo = (sum_att - hi.astype(f32)).astype(bf16)
    pooled = (sum_tok + dot(hi, wo_ref[...]) + dot(lo, wo_ref[...])) * (1.0 / patches)
    centred = pooled - jnp.mean(pooled, axis=1, keepdims=True)
    inv = lax.rsqrt(jnp.mean(centred * centred, axis=1, keepdims=True) + epsilon)
    plain = centred * inv
    frame = (plain * gain_ref[...]).astype(bf16)
    wide_ref[0] = frame.astype(f32)
    logits = dot(frame, wg_ref[...], ((1,), (1,)))
    padded, vocab = logits.shape
    raised = jnp.exp(logits)
    denom = jnp.sum(raised, axis=1, keepdims=True)
    soft = raised / denom
    logs = logits - jnp.log(denom)
    cap = labels_ref.shape[1]
    length = length_ref[0]
    lane = lax.broadcasted_iota(jnp.int32, (1, 128), 1)
    gloss = lax.broadcasted_iota(jnp.int32, (padded, vocab), 1)

    def pick(label):
        return jnp.sum(jnp.where(gloss == label, logs, 0.0), axis=1, keepdims=True)

    wide = lax.broadcasted_iota(jnp.int32, (padded, 128), 1)
    emitted = jnp.where((wide & 1) == 0, pick(0), 0.0)
    skip = lane < 0
    for i in range(cap):
        label = labels_ref[0, i]
        emitted = jnp.where(wide == 2 * i + 1, pick(label), emitted)
        before = labels_ref[0, i - 1] if i else -1
        skip = skip | ((lane == 2 * i + 1) & (label != before))
    usable = lane < 2 * length + 1
    start = (lane < 2) & usable
    alphas = jnp.where(start, emitted[0:1], very_low)
    kept = []
    for t in range(1, frames):
        one = jnp.where(lane < 1, very_low, pltpu.roll(alphas, 1, 1))
        two = jnp.where(skip, pltpu.roll(alphas, 2, 1), very_low)
        outer = add_log(add_log(alphas, one), two)
        kept.append((jnp.exp(alphas - outer), jnp.exp(one - outer), jnp.exp(two - outer)))
        alphas = jnp.where(usable, outer + emitted[t : t + 1], very_low)
    last = jnp.sum(jnp.where(lane == 2 * length, alphas, 0.0), axis=1, keepdims=True)
    prior = jnp.sum(jnp.where(lane == 2 * length - 1, alphas, 0.0), axis=1, keepdims=True)
    ending = add_log(last, prior)
    share = 1.0 / length.astype(f32)
    loss_ref[...] = jnp.broadcast_to(-ending * share, (8, 128))
    grad = jnp.where(
        (lane == 2 * length) | (lane == 2 * length - 1), -share * jnp.exp(alphas - ending), 0.0
    )
    row = lax.broadcasted_iota(jnp.int32, (padded, 128), 0)
    emit_grad = jnp.zeros((padded, 128), f32)
    for t in range(frames - 1, 0, -1):
        grad = jnp.where(usable, grad, 0.0)
        emit_grad = jnp.where(row == t, grad, emit_grad)
        w_own, w_one, w_two = kept[t - 1]
        from_one = jnp.where(lane < 1, 0.0, grad * w_one)
        from_two = jnp.where(skip, grad * w_two, 0.0)
        from_two = jnp.where(lane < 2, 0.0, from_two)
        grad = grad * w_own + pltpu.roll(from_one, 127, 1) + pltpu.roll(from_two, 126, 1)
    emit_grad = jnp.where(row == 0, jnp.where(start, grad, 0.0), emit_grad)
    blank = jnp.sum(jnp.where((wide & 1) == 0, emit_grad, 0.0), axis=1, keepdims=True)
    d_logs = jnp.where(gloss == 0, blank, 0.0)
    for i in range(cap):
        part = jnp.sum(jnp.where(wide == 2 * i + 1, emit_grad, 0.0), axis=1, keepdims=True)
        d_logs = d_logs + jnp.where(gloss == labels_ref[0, i], part, 0.0)
    d_logits = d_logs - soft * jnp.sum(emit_grad, axis=1, keepdims=True)
    gl = d_logits.astype(bf16)
    packed_ref[:, 2 * width + 3 * step :] = gl
    grad_frame = dot(gl, wg_ref[...])
    head = jnp.sum(grad_frame * plain, axis=0, keepdims=True)
    first_row = lax.broadcasted_iota(jnp.int32, (padded, width), 0) == 0
    wide_ref[2] = jnp.where(first_row, jnp.broadcast_to(head, (padded, width)), 0.0)
    start_at = lax.axis_index("seq") * block
    for i in range(3):
        part = wide_ref[i, :, pl.ds(pl.multiple_of(start_at // 128 * 128, 128), step)]
        for shift in range(block, 128, block):
            part = jnp.where(lax.rem(start_at, 128) == shift, pltpu.roll(part, 128 - shift, 1), part)
        packed_ref[:, 2 * width + i * step : 2 * width + (i + 1) * step] = part.astype(bf16)
    scaled = grad_frame * gain_ref[...]
    grad_pooled = inv * (
        scaled
        - jnp.mean(scaled, axis=1, keepdims=True)
        - plain * jnp.mean(scaled * plain, axis=1, keepdims=True)
    )
    grad_mixed = grad_pooled * (1.0 / patches)
    mix_ref[...] = grad_mixed
    mixed_low = grad_mixed.astype(bf16)
    packed_ref[:, :width] = mixed_low
    ga = dot(mixed_low, wo_ref[...], ((1,), (1,))).astype(bf16)
    ga_ref[...] = ga
    packed_ref[:, width : 2 * width] = ga


def backward_kernel(
    patches, frames, here, q_ref, k_ref, v_ref, p_ref, low_ref, norm_ref, inv_ref, ga_ref, mix_ref,
    gain_ref, w_ref, gt_ref, dw_ref, cols_ref, qk_ref,
):
    rows, width = q_ref.shape
    head_lanes = p_ref.shape[1]
    ga = by_head(ga_ref[...].astype(f32)[:frames], head_lanes).astype(bf16)
    probs = p_ref[...]
    probs_low = probs.astype(bf16)
    grad_probs = dot(v_ref[...], ga, ((1,), (1,)))
    inner = jnp.sum((grad_probs * probs).reshape(frames, here, head_lanes), axis=0, keepdims=True)
    grad_scores = probs.reshape(frames, here, head_lanes) * (
        grad_probs.reshape(frames, here, head_lanes) - inner
    )
    scores_low = (grad_scores.reshape(rows, head_lanes) * SCALE).astype(bf16)
    low = low_lanes(rows)
    for pair in range(H // 2):
        at = slice(pair * 128, (pair + 1) * 128)
        keys = k_ref[:, at].astype(f32).reshape(frames, here, 128)
        grad_keys = jnp.zeros((frames, here, 128), f32)
        queries = []
        for t in range(frames):
            wide = dot(scores_low, spread(head_lanes, 128, pair * 128, t)).reshape(frames, here, 128)
            queries.append(jnp.sum(wide * keys, axis=0))
            q_t = q_ref[t * here : (t + 1) * here, at].astype(f32)
            grad_keys += wide * q_t[None]
        gq = jnp.concatenate(queries, axis=0)
        gk = pltpu.roll(grad_keys.reshape(rows, 128), HD, 1)
        gv = dot(probs_low, ga[:, at])
        qk_ref[:, pair * 256 : pair * 256 + 128] = gq.astype(bf16)
        qk_ref[:, pair * 256 + 128 : pair * 256 + 256] = gk.astype(bf16)
        a = jnp.where(low, gq, gk).astype(bf16)
        b = jnp.where(low, gv, gq).astype(bf16)
        c = jnp.where(low, gk, gv).astype(bf16)
        part = dot(
            jnp.concatenate([a, b, c], axis=1), w_ref[:, pair * 384 : (pair + 1) * 384], ((1,), (1,))
        )
        if pair == 0:
            grad_normed = part
        else:
            grad_normed += part
    tokens_low = low_ref[...]
    chunk = 512
    for start in range(0, 2 * width, chunk):
        dw_ref[:, start : start + chunk] = dot(
            tokens_low, qk_ref[:, start : start + chunk], ((0,), (0,))
        ).astype(bf16)
    coefs = dot(tokens_low, probs_low, ((0,), (0,)))
    normed = norm_ref[...]
    gain_part = (grad_normed * normed).astype(bf16)
    gain_cols = dot(gain_part, jnp.ones((rows, 128), bf16), ((0,), (0,)))
    if frames * H < head_lanes:
        lane = lax.broadcasted_iota(jnp.int32, (width, 128), 1)
        tail = head_lanes - 128
        if tail:
            cols_ref[:, :tail] = coefs[:, :tail].astype(bf16)
        cols_ref[:, tail:] = jnp.where(lane < frames * H - tail, coefs[:, tail:], gain_cols).astype(bf16)
    else:
        cols_ref[:, :head_lanes] = coefs.astype(bf16)
        cols_ref[:, head_lanes:] = gain_cols.astype(bf16)
    scaled = grad_normed * gain_ref[...]
    back = inv_ref[:, :1] * (
        scaled
        - jnp.mean(scaled, axis=1, keepdims=True)
        - normed * jnp.mean(scaled * normed, axis=1, keepdims=True)
    )
    for t in range(frames):
        gt_ref[t] = ((back[t * here : (t + 1) * here] + mix_ref[t : t + 1, :]) * patches).astype(bf16)


def final_kernel(
    frames, qk_ref, cols_ref, rows_ref,
    qkv_out, out_out, gloss_out, head_out, gain_out,
):
    clips, block, lanes = cols_ref.shape
    head_lanes = up(frames * H, 128)
    padded = rows_ref.shape[1]
    width, vocab = out_out.shape[1], gloss_out.shape[0]
    step = up(block, 128)

    def part(start, size):
        return rows_ref[:, :, start : start + size].astype(f32).reshape(clips * padded, size)

    at = 2 * width
    frame, att, head = [part(at + i * step, step)[:, :block] for i in range(3)]
    out_out[...] = dot(att.astype(bf16), part(0, width).astype(bf16), ((0,), (0,)))
    gloss_out[...] = dot(
        part(at + 3 * step, vocab).astype(bf16), frame.astype(bf16), ((0,), (0,))
    )
    head_out[...] = jnp.sum(head, axis=0, keepdims=True)
    gains = jnp.sum(cols_ref[:, :, lanes - 128 :].astype(f32), axis=0)
    gain_out[...] = jnp.transpose(gains)[127:128]
    values = None
    for c in range(clips):
        ga = by_head(rows_ref[c, :, width : 2 * width].astype(f32)[:frames], head_lanes).astype(bf16)
        part = dot(cols_ref[c, :, :head_lanes], ga)
        values = part if values is None else values + part
    low = low_lanes(block)
    for pair in range(H // 2):
        q = qk_ref[:, pair * 256 : pair * 256 + 128].astype(f32)
        k = qk_ref[:, pair * 256 + 128 : pair * 256 + 256].astype(f32)
        v = values[:, pair * 128 : (pair + 1) * 128]
        qkv_out[:, pair * 384 : pair * 384 + 128] = jnp.where(low, q, k)
        qkv_out[:, pair * 384 + 128 : pair * 384 + 256] = jnp.where(low, v, q)
        qkv_out[:, pair * 384 + 256 : pair * 384 + 384] = jnp.where(low, k, v)


def exchange_scratch(seq_count, clips, block, width, lanes, chunk_count):
    pairs, half = seq_count // 2, clips // 2
    wide = 2 * width + lanes
    piece = 2 * width // clips
    sems = pltpu.SemaphoreType.DMA
    return [
        pltpu.VMEM((pairs, block, wide), bf16),
        pltpu.VMEM((pairs, block, wide), bf16),
        pltpu.VMEM((pairs - 1, block, wide), bf16),
        pltpu.VMEM((block, wide), bf16),
        pltpu.VMEM((block, width), bf16),
        pltpu.VMEM((block, width), bf16),
        pltpu.VMEM((half - 1, block, piece), bf16),
        sems((2, seq_count - 1)),
        sems((2, half)),
        sems((2, chunk_count, 2 * pairs)),
        sems((2, chunk_count, pairs - 1)),
        sems((2, chunk_count)),
        sems((2, chunk_count, half - 1)),
        sems((2, chunk_count, half - 1)),
        sems((2, chunk_count, half - 1)),
        sems((2, chunk_count, 2)),
    ]


def exchange_kernel(
    chunk_count, dw_ref, cols_ref, rows_ref, gt_ref, sum_ref, all_cols_ref, all_rows_ref, back_ref,
    core_in, core_sum, pair_in, seq_sum, x_in, x_sum, z_in,
    token_sem, row_sem, core_sem, pair_sem, x_sem, z_sem, zq_sem, zc_sem, xg_sem,
):
    seq_count, local = back_ref.shape[:2]
    half = all_cols_ref.shape[1]
    pairs = seq_count // 2
    block, full = sum_ref.shape
    width = full // 2
    piece = width // half
    size = block // chunk_count
    me = lax.axis_index("seq")
    clip = lax.axis_index("clip")
    core, hi = lax.rem(me, 2), me // 2
    x, z = lax.rem(clip, 2), clip // 2

    def at(clip_id, seq_id):
        return (clip_id, seq_id)

    sibling = at(clip, hi * 2 + (1 - core))
    x_peer = at(z * 2 + (1 - x), me)

    def z_peer(step):
        return at(lax.rem(z + step, half) * 2 + x, me)

    barrier = pltpu.get_barrier_semaphore()
    peers = [at(clip, lax.rem(me + step, seq_count)) for step in range(1, seq_count)]
    peers += [x_peer] + [z_peer(step) for step in range(1, half)]
    for peer in peers:
        pl.semaphore_signal(barrier, inc=1, device_id=peer, device_id_type=pl.DeviceIdType.MESH)
    pl.semaphore_wait(barrier, len(peers))

    started = []

    def send(src, dst, sems, index, peer):
        copy = pltpu.make_async_remote_copy(
            src_ref=src,
            dst_ref=dst,
            send_sem=sems.at[(0,) + index],
            recv_sem=sems.at[(1,) + index],
            device_id=peer,
            device_id_type=pl.DeviceIdType.MESH,
        )
        copy.start()
        started.append(copy)
        return copy

    waits = {}

    def rows(c):
        return pl.ds(c * size, size)

    def block_rows(index, c):
        return pl.ds(pl.multiple_of(index * block + c * size, 16), size)

    def half_cols(index):
        return pl.ds(pl.multiple_of(index * width, 128), width)

    def first(c):
        waits[1, c] = []
        for p in range(pairs):
            src = block_rows(p * 2 + (1 - core), c)
            waits[1, c] += [
                send(dw_ref.at[src], core_in.at[p, rows(c), pl.ds(0, full)], core_sem, (c, 2 * p), sibling),
                send(
                    cols_ref.at[src],
                    core_in.at[p, rows(c), pl.ds(full, cols_ref.shape[1])],
                    core_sem,
                    (c, 2 * p + 1),
                    sibling,
                ),
            ]

    def second(c):
        for copy in waits[1, c]:
            copy.wait_recv()
        for p in range(pairs):
            own = block_rows(p * 2 + core, c)
            core_sum[p, rows(c), :full] = dw_ref[own, :] + core_in[p, rows(c), :full]
            core_sum[p, rows(c), full:] = cols_ref[own, :] + core_in[p, rows(c), full:]
        waits[2, c] = [
            send(
                core_sum.at[lax.rem(hi + step, pairs), rows(c)],
                pair_in.at[step - 1, rows(c)],
                pair_sem,
                (c, step - 1),
                at(clip, lax.rem(hi + step, pairs) * 2 + core),
            )
            for step in range(1, pairs)
        ]

    def third(c):
        for copy in waits[2, c]:
            copy.wait_recv()
        total = core_sum[hi, rows(c)].astype(f32)
        for step in range(pairs - 1):
            total += pair_in[step, rows(c)].astype(f32)
        total = total.astype(bf16)
        seq_sum[rows(c)] = total
        all_cols_ref[x, z, rows(c)] = total[:, full:]
        waits[3, c] = [
            send(seq_sum.at[rows(c), half_cols(1 - x)], x_in.at[rows(c)], x_sem, (c,), x_peer)
        ]
        waits[5, c] = [
            send(
                all_cols_ref.at[x, z, rows(c)],
                all_cols_ref.at[x, z, rows(c)],
                zc_sem,
                (c, step - 1),
                z_peer(step),
            )
            for step in range(1, half)
        ]

    def fourth(c):
        for copy in waits[3, c]:
            copy.wait_recv()
        x_sum[rows(c)] = seq_sum[rows(c), half_cols(x)] + x_in[rows(c)]
        waits[4, c] = [
            send(
                x_sum.at[rows(c), pl.ds(pl.multiple_of(lax.rem(z + step, half) * piece, 128), piece)],
                z_in.at[step - 1, rows(c)],
                z_sem,
                (c, step - 1),
                z_peer(step),
            )
            for step in range(1, half)
        ]

    def fifth(c):
        for copy in waits[4, c]:
            copy.wait_recv()
        total = x_sum[rows(c), pl.ds(pl.multiple_of(z * piece, 128), piece)].astype(f32)
        for step in range(half - 1):
            total += z_in[step, rows(c)].astype(f32)
        own = pl.ds(pl.multiple_of(x * width + z * piece, 128), piece)
        sum_ref[rows(c), own] = total.astype(bf16)
        waits[5, c] += [
            send(
                sum_ref.at[rows(c), own], sum_ref.at[rows(c), own], zq_sem, (c, step - 1), z_peer(step)
            )
            for step in range(1, half)
        ]

    def sixth(c):
        for copy in waits[5, c]:
            copy.wait_recv()
        mine = (rows(c), half_cols(x))
        waits[6, c] = [
            send(sum_ref.at[mine], sum_ref.at[mine], xg_sem, (c, 0), x_peer),
            send(
                all_cols_ref.at[x, :, rows(c)], all_cols_ref.at[x, :, rows(c)], xg_sem, (c, 1), x_peer
            ),
        ]

    def seventh(c):
        for copy in waits[6, c]:
            copy.wait_recv()

    stages = [first, second, third, fourth, fifth, sixth, seventh]
    for c in range(chunk_count):
        first(c)
    for c in range(chunk_count):
        second(c)
    all_rows_ref[x, z] = rows_ref[...]
    row_waits = [
        send(rows_ref, all_rows_ref.at[x, z], row_sem, (step - 1,), z_peer(step))
        for step in range(1, half)
    ]
    token_waits = []
    for step in range(1, seq_count):
        to = lax.rem(me + step, seq_count)
        token_waits.append(
            send(gt_ref.at[pl.ds(to * local, local)], back_ref.at[me], token_sem, (step - 1,), at(clip, to))
        )
    back_ref[me] = gt_ref[pl.ds(me * local, local)]
    for wave in range(2, chunk_count + len(stages) - 1):
        for c in range(chunk_count):
            if 2 <= wave - c < len(stages):
                stages[wave - c](c)
        if wave == 3:
            for copy in row_waits:
                copy.wait_recv()
            row_waits = [send(all_rows_ref.at[x], all_rows_ref.at[x], row_sem, (half - 1,), x_peer)]
    for copy in row_waits + token_waits:
        copy.wait_recv()
    for copy in started:
        copy.wait_send()


def params():
    return pltpu.CompilerParams(vmem_limit_bytes=56 << 20)


def shape(dims, kind):
    return jax.ShapeDtypeStruct(dims, kind)


VM = pl.BlockSpec(memory_space=pltpu.VMEM)
SM = pl.BlockSpec(memory_space=pltpu.SMEM)


def per_device(
    clip_tokens, attn_gain, qkv_weight, out_weight, head_gain, gloss_weight, gloss_targets, target_lengths
):
    seq_count = lax.axis_size("seq")
    clips = lax.axis_size("clip")
    me = lax.axis_index("seq")
    local, patches, width = clip_tokens.shape[1:]
    vocab = gloss_weight.shape[1]
    frames = local * seq_count
    here = up(-(-patches // seq_count), 16)
    rows = frames * here
    head_lanes = up(frames * H, 128)
    lanes = up(frames * H + 1, 128)
    padded = up(frames, 8)
    block = width // seq_count
    gain_row = attn_gain.reshape(1, width)

    own = jnp.pad(clip_tokens[0], ((0, 0), (0, here * seq_count - patches), (0, 0)))
    q, k, v, probs, low, normed, inv, all_sums = pl.pallas_call(
        forward_kernel,
        out_shape=(
            shape((rows, width), bf16),
            shape((rows, width), bf16),
            shape((rows, width), bf16),
            shape((rows, head_lanes), f32),
            shape((rows, width), bf16),
            shape((rows, width), f32),
            shape((rows, 128), f32),
            shape((seq_count, 2, padded, width), f32),
        ),
        in_specs=[VM, VM, pl.BlockSpec(memory_space=pl.ANY)],
        out_specs=(VM,) * 8,
        scratch_shapes=[
            pltpu.VMEM((frames, here, width), bf16),
            pltpu.VMEM(qkv_weight.shape, bf16),
            pltpu.SemaphoreType.DMA,
            pltpu.SemaphoreType.DMA((2, seq_count - 1)),
            pltpu.SemaphoreType.DMA((2, seq_count - 1)),
        ],
        compiler_params=pltpu.CompilerParams(
            vmem_limit_bytes=56 << 20, collective_id=1, has_side_effects=True
        ),
        name="forward",
    )(own, gain_row, qkv_weight)
    loss, packed, grad_mixed, ga = pl.pallas_call(
        functools.partial(middle_kernel, patches, frames),
        out_shape=(
            shape((8, 128), f32),
            shape((padded, 2 * width + 3 * up(block, 128) + vocab), bf16),
            shape((padded, width), f32),
            shape((padded, width), bf16),
        ),
        in_specs=[SM, SM] + [VM] * 4,
        out_specs=(VM,) * 4,
        scratch_shapes=[pltpu.VMEM((3, padded, width), f32)],
        compiler_params=params(),
        name="middle",
    )(gloss_targets, target_lengths, all_sums, out_weight, head_gain.reshape(1, width), gloss_weight.T)

    gt, dw, cols = pl.pallas_call(
        functools.partial(backward_kernel, patches, frames, here),
        out_shape=(
            shape((frames, here, width), bf16),
            shape((width, 2 * width), bf16),
            shape((width, lanes), bf16),
        ),
        in_specs=[VM] * 11,
        out_specs=(VM,) * 3,
        scratch_shapes=[pltpu.VMEM((rows, 2 * width), bf16)],
        compiler_params=params(),
        name="backward",
    )(q, k, v, probs, low, normed, inv, ga, grad_mixed, gain_row, qkv_weight)
    half = clips // 2
    chunk_count = 4
    dw_sum, cols_all, gathered, back = pl.pallas_call(
        functools.partial(exchange_kernel, chunk_count),
        out_shape=(
            shape((block, 2 * width), bf16),
            shape((2, half, block, lanes), bf16),
            shape((2, half) + packed.shape, bf16),
            shape((seq_count, local, here, width), bf16),
        ),
        in_specs=[VM] * 4,
        out_specs=(VM,) * 4,
        scratch_shapes=exchange_scratch(seq_count, clips, block, width, lanes, chunk_count),
        compiler_params=pltpu.CompilerParams(
            vmem_limit_bytes=56 << 20, collective_id=0, has_side_effects=True
        ),
        name="exchange",
    )(dw, cols, packed, gt)
    cols_all = cols_all.reshape(clips, block, lanes)
    gathered = gathered.reshape((clips,) + packed.shape)
    back = back.transpose(1, 0, 2, 3).reshape(local, seq_count * here, width)
    grad_tokens = back[None, :, :patches]

    qkv_share, out_share, gloss_share, head_share, gain_share = pl.pallas_call(
        functools.partial(final_kernel, frames),
        out_shape=(
            shape((block, 3 * width), f32),
            shape((block, width), f32),
            shape((vocab, block), f32),
            shape((1, block), f32),
            shape((1, block), f32),
        ),
        in_specs=[VM] * 3,
        out_specs=(VM,) * 5,
        compiler_params=params(),
        name="final",
    )(dw_sum, cols_all, gathered)
    return (
        loss[0, :1],
        grad_tokens,
        gain_share[0],
        qkv_share,
        out_share,
        head_share[0],
        gloss_share.T,
    )


def solution(mesh):
    in_specs = (P("clip", "seq", None, None), P(), P(), P(), P(), P(), P("clip", None), P("clip"))
    out_specs = (
        P("clip"),
        P("clip", "seq", None, None),
        P("seq"),
        P("seq", None),
        P("seq", None),
        P("seq"),
        P("seq", None),
    )
    return jax.shard_map(
        per_device, mesh=mesh, in_specs=in_specs, out_specs=out_specs, check_vma=False
    )
```
